256 devices in a mesh: comp: 2 (over core), blk: 128 (over x, y, z).
Axes of the slice: x: 4, y: 4, z: 8, core: 2. Of those that a mesh axis runs over, the one named last changes fastest.
Arguments:
- conserved: float32 [2, 8, 8192, 512], P('comp', None, 'blk'), may hold values from -3 to 10, as said below
- block_rate: float32 [2, 8192], P('comp', 'blk'), may hold values from 0.004 to 0.016
- neighbours: int32 [2, 8192, 6], P('comp', 'blk'), may hold values from -1 to 8191, as said below
- shell_cell: int32 [2, 128, 128, 32], P('comp', 'blk'), may hold values from 0 to 32694, as said below
- shell_frac: float32 [2, 3, 128, 128, 32], P('comp', None, 'blk'), may hold values from 0 to 1
- shell_target: int32 [2, 128, 128, 32], P('comp', 'blk'), may hold values from 0 to 32768, as said below
Outputs:
- new_state: float32 [2, 8, 8192, 512], P('comp', None, 'blk')
The draws below stay inside these ranges and needn't reach their ends.
Inputs may be any that keep to these rules, and one draw needn't show every extreme that they name: `conserved`: cells of states whose density and pressure lie between 0.5 and 2 and whose speeds and field components are of order one, with total energy = pressure / (5/3 - 1) + kinetic + magnetic energy. Face neighbours are mutual: if block h is the high-side neighbour of g along an axis, g is the low-side neighbour of h. A neighbour lies on the same device or at most 4 devices away along blk. For each component, axis and each k in -4..-1, 1..4, exactly 3 local block positions of every device have their high-side neighbour k devices away (the same positions on every device); the neighbour is -1 where that device does not exist. So a device sends exactly 18 faces to each device k places away when both exist. `shell_cell`: each stencil lies inside one block: the corner cell has coordinates 0 to 6 along every axis. `shell_target`: for each target component, the used slots of one target device name distinct cells of its blocks, and used slots come first in each row. Every source device fills all 32 slots towards a few target devices and at least half of them towards each of the others.
All inputs are finite; a program needn't handle non-finite values.
Results may differ from the reference program's by a relative error of at most 0.0003.
Values sent between devices are 32-bit elements; how exact they have to be, the bound alone decides.
A program may use at most 256 MiB of HBM per device.

```python
import math
import jax
import jax.numpy as jnp
import numpy as np
from jax import lax

BLK_DEV = 64
STEPS = 3
REACH = 4
PAIRS = 3
SHELL_SLOTS = 32
BLOCKS = 8192
N_BLK = 128


GAMMA = 5.0 / 3.0


def draw_conserved(key, part):
    extent = (2, BLOCKS, 512)
    key_list = jax.random.split(jax.random.fold_in(key, 7), 4)
    density = jnp.exp(jax.random.uniform(key_list[0], extent, minval=jnp.log(0.5), maxval=jnp.log(2.0)))
    pressure = jnp.exp(jax.random.uniform(key_list[1], extent, minval=jnp.log(0.5), maxval=jnp.log(2.0)))
    velocity = 0.4 * jax.random.truncated_normal(key_list[2], -2.5, 2.5, (3,) + extent)
    magnetic_field = 0.5 * jax.random.truncated_normal(key_list[3], -2.5, 2.5, (3,) + extent)
    momentum = density[None] * velocity
    energy = pressure / (GAMMA - 1.0) + 0.5 * density * jnp.sum(velocity * velocity, axis=0) + 0.5 * jnp.sum(magnetic_field * magnetic_field, axis=0)
    stacked = jnp.concatenate([density[None], momentum, magnetic_field, energy[None]], axis=0)
    return stacked.transpose(1, 0, 2, 3).astype(jnp.float32)


def draw_neighbours(key, part):
    number = BLK_DEV
    devices = N_BLK
    offsets = jnp.concatenate([jnp.arange(-REACH, 0, dtype=jnp.int32), jnp.arange(1, REACH + 1, dtype=jnp.int32)])
    pattern = jnp.concatenate([jnp.repeat(offsets, PAIRS), jnp.zeros((number - 2 * REACH * PAIRS,), jnp.int32)])
    result = jnp.zeros((2, devices * number, 6), jnp.int32)
    device_ids = jnp.arange(devices, dtype=jnp.int32)[:, None]
    local_index = jnp.arange(number, dtype=jnp.int32)[None, :]
    for component in range(2):
        for d in range(3):
            subkey = jax.random.fold_in(key, 17 * component + d + 3)
            key_list = jax.random.split(subkey, devices + 1)
            shifts = jax.random.permutation(key_list[0], pattern)
            mixings = jax.vmap(lambda k: jax.random.permutation(k, number))(key_list[1:]).astype(jnp.int32)
            target = device_ids + shifts[None, :]
            inside = (target >= 0) & (target < devices)
            clipped = jnp.clip(target, 0, devices - 1)
            landing = mixings[clipped, jnp.broadcast_to(local_index, clipped.shape)]
            upper_link = jnp.where(inside, clipped * number + landing, -1).reshape(-1)
            sources = (device_ids * number + local_index).reshape(-1)
            lower_link = jnp.full((devices * number,), -1, jnp.int32).at[jnp.where(upper_link >= 0, upper_link, devices * number)].set(sources, mode='drop')
            result = result.at[component, :, 2 * d + 1].set(upper_link).at[component, :, 2 * d].set(lower_link)
    return result


def draw_shell_cell(key, part):
    extent = (2, N_BLK, N_BLK, SHELL_SLOTS)
    key_list = jax.random.split(jax.random.fold_in(key, 29), 4)
    block_index = jax.random.randint(key_list[0], extent, 0, BLK_DEV)
    corner = [jax.random.randint(key_list[1 + j], extent, 0, 7) for j in range(3)]
    cells = (block_index * 512 + corner[0] * 64 + corner[1] * 8 + corner[2]).astype(jnp.int32)
    cells = cells.at[0, 0, 0, 0].set((BLK_DEV - 1) * 512 + 438).at[0, 0, 0, 1].set(0)
    return cells.astype(jnp.int32)


def target_one(key):
    devices = N_BLK
    cells_here = BLK_DEV * 512
    key_list = jax.random.split(key, 3)
    busy_set = jax.random.permutation(key_list[0], devices) < max(devices // 8, 1)
    counts = jax.random.randint(key_list[1], (devices, devices), SHELL_SLOTS // 2, SHELL_SLOTS + 1)
    counts = jnp.where(busy_set[:, None], SHELL_SLOTS, counts)
    chosen = jax.vmap(lambda k: jax.random.permutation(k, cells_here)[:devices * SHELL_SLOTS])(jax.random.split(key_list[2], devices))
    chosen = chosen.reshape(devices, devices, SHELL_SLOTS)
    in_use = jnp.arange(SHELL_SLOTS)[None, None, :] < counts[:, :, None]
    return jnp.where(in_use, chosen, cells_here).astype(jnp.int32)


def draw_shell_target(key, part):
    return jnp.stack([target_one(jax.random.fold_in(key, 41 + component)) for component in range(2)]).astype(jnp.int32)


def shard_levels(stream_key, dims, cuts, low, high):
    loudness, own = 1.0, jax.random.fold_in(stream_key, 6)
    for dim, shards_of in cuts:
        steps = jnp.exp(jax.random.uniform(jax.random.fold_in(own, dim), (shards_of,), jnp.float32, low / len(cuts), high / len(cuts)))
        loudness = loudness * jnp.repeat(steps, dims[dim] // shards_of).reshape([-1 if axis == dim else 1 for axis in range(len(dims))])
    return loudness


def setup_inputs(seed: int = 0) -> dict:
    keys = jax.random.split(jax.random.key(seed), 7)
    conserved = draw_conserved(jax.random.fold_in(keys[6], 71), 0)
    block_rate = jnp.clip(jnp.exp(math.log(0.016) - 1.3862944 * jax.random.uniform(keys[1], (2, BLOCKS), jnp.float32) ** shard_levels(keys[1], (2, BLOCKS), ((0, 2), (1, 128)), -0.2, 0.2)), 0.004, 0.016)
    neighbours = draw_neighbours(jax.random.fold_in(keys[6], 71), 0)
    shell_cell = draw_shell_cell(jax.random.fold_in(keys[6], 71), 0)
    shell_frac = jnp.clip(1.0 * jax.random.uniform(keys[4], (2, 3, N_BLK, N_BLK, SHELL_SLOTS), jnp.float32) ** shard_levels(keys[4], (2, 3, N_BLK, N_BLK, SHELL_SLOTS), ((0, 2), (2, 128)), -0.2, 0.2), 0.0, 1.0)
    shell_target = draw_shell_target(jax.random.fold_in(keys[6], 71), 0)
    return dict(conserved=conserved, block_rate=block_rate, neighbours=neighbours, shell_cell=shell_cell, shell_frac=shell_frac, shell_target=shell_target)


GAMMA = 5.0 / 3.0

def cell_layout():
    position = np.arange(512)
    coords = [position // 64, position // 8 % 8, position % 8]
    spreads = [position % 64, position // 64 * 8 + position % 8, position // 8]
    return (coords, spreads)

def wave_flux(u, d):
    inverse = 1.0 / u[0]
    velocity = [u[1] * inverse, u[2] * inverse, u[3] * inverse]
    magnetic_field = [u[4], u[5], u[6]]
    kinetic = 0.5 * (u[1] * velocity[0] + u[2] * velocity[1] + u[3] * velocity[2])
    magnetic = 0.5 * (u[4] * u[4] + u[5] * u[5] + u[6] * u[6])
    pressure = (GAMMA - 1.0) * (u[7] - kinetic - magnetic)
    summed = pressure + magnetic
    normal = velocity[d]
    normal_field = magnetic_field[d]
    alignment = velocity[0] * u[4] + velocity[1] * u[5] + velocity[2] * u[6]
    components = [u[1 + d]]
    for j in range(3):
        component = u[1 + j] * normal - magnetic_field[j] * normal_field
        if j == d:
            component = component + summed
        components.append(component)
    for j in range(3):
        components.append(normal * magnetic_field[j] - normal_field * velocity[j])
    components.append((u[7] + summed) * normal - normal_field * alignment)
    sound_sq = GAMMA * pressure * inverse
    alfven = 2.0 * magnetic * inverse
    combined = sound_sq + alfven
    fast_speed = jnp.sqrt(0.5 * (combined + jnp.sqrt(combined * combined - 4.0 * sound_sq * normal_field * normal_field * inverse)))
    return (jnp.stack(components), jnp.abs(normal) + fast_speed)

def collect_faces(current):
    coords, _ = cell_layout()
    position = np.arange(512)
    number = current.shape[1]
    pieces = []
    for f in range(6):
        where_cells = position[coords[f // 2] == 7 * (f % 2)]
        pieces.append(jnp.take(current, where_cells, axis=2).transpose(1, 0, 2).reshape(number, 512))
    return jnp.concatenate(pieces, axis=0)

def advance(current, ghost_rows, block_rate):
    coords, spreads = cell_layout()
    position = np.arange(512)
    number = current.shape[1]
    ghosts = ghost_rows.reshape(6, number, 8, 64).transpose(0, 2, 1, 3)
    strides = [64, 8, 1]
    change = jnp.zeros_like(current)
    for d in range(3):
        at_low = jnp.asarray(coords[d] == 0)
        at_high = jnp.asarray(coords[d] == 7)
        low_cells = position[coords[d] == 0]
        spread = spreads[d]
        flux_here, speed_here = wave_flux(current, d)
        ghost_low = ghosts[2 * d]
        ghost_high = ghosts[2 * d + 1]
        flux_low, speed_low = wave_flux(ghost_low, d)
        flux_high, speed_high = wave_flux(ghost_high, d)
        right_state = jnp.where(at_high, jnp.take(ghost_high, spread, axis=2), jnp.roll(current, -strides[d], axis=2))
        right_flux = jnp.where(at_high, jnp.take(flux_high, spread, axis=2), jnp.roll(flux_here, -strides[d], axis=2))
        right_speed = jnp.where(at_high, jnp.take(speed_high, spread, axis=1), jnp.roll(speed_here, -strides[d], axis=1))
        upper_flux = 0.5 * (flux_here + right_flux) - 0.5 * jnp.maximum(speed_here, right_speed) * (right_state - current)
        face_state = jnp.take(current, low_cells, axis=2)
        face_flux = jnp.take(flux_here, low_cells, axis=2)
        face_speed = jnp.take(speed_here, low_cells, axis=1)
        edge_flux = 0.5 * (flux_low + face_flux) - 0.5 * jnp.maximum(speed_low, face_speed) * (face_state - ghost_low)
        lower_flux = jnp.where(at_low, jnp.take(edge_flux, spread, axis=2), jnp.roll(upper_flux, strides[d], axis=2))
        change = change + (upper_flux - lower_flux)
    return current - block_rate[None, :, None] * change

def interpolate(flattened, cell_index, fractions):
    summed = None
    for a in range(2):
        for b in range(2):
            for c in range(2):
                weight = (fractions[0] if a else 1.0 - fractions[0]) * (fractions[1] if b else 1.0 - fractions[1]) * (fractions[2] if c else 1.0 - fractions[2])
                corner = weight * jnp.take(flattened, cell_index + (64 * a + 8 * b + c), axis=1)
                summed = corner if summed is None else summed + corner
    return summed

def ghost_rows_of(current, links):
    number = current.shape[1]
    face_table = collect_faces(current)
    face_ids = jnp.arange(6, dtype=jnp.int32)[:, None]
    blocks = jnp.arange(number, dtype=jnp.int32)[None, :]
    partner = links.T
    source = jnp.where(partner >= 0, jnp.bitwise_xor(face_ids, 1) * number + partner, face_ids * number + blocks)
    return jnp.take(face_table, source.reshape(-1), axis=0)

def advance_all(current, ghost_rows, block_rate):
    number = current.shape[1]
    groups = number // BLK_DEV
    fields = current.reshape(8, groups, BLK_DEV, 512).transpose(1, 0, 2, 3)
    ghost_groups = ghost_rows.reshape(6, groups, BLK_DEV, 512).transpose(1, 0, 2, 3).reshape(groups, 6 * BLK_DEV, 512)
    rate_groups = block_rate.reshape(groups, BLK_DEV)
    advanced = lax.map(lambda bundle: advance(bundle[0], bundle[1], bundle[2]), (fields, ghost_groups, rate_groups))
    return advanced.transpose(1, 0, 2, 3).reshape(8, number, 512)

def reference(conserved, block_rate, neighbours, shell_cell, shell_frac, shell_target):
    span = BLK_DEV * 512
    devices = jnp.arange(N_BLK, dtype=jnp.int32)[:, None, None]
    starts = []
    for target in range(2):
        source = 1 - target
        source_flat = conserved[source].reshape(8, BLOCKS * 512)
        values = interpolate(source_flat, shell_cell[source] + devices * span, shell_frac[source])
        places = jnp.where(shell_target[target] < span, shell_target[target] + devices * span, BLOCKS * 512)
        ordered = values.transpose(0, 2, 1, 3).reshape(8, -1)
        target_flat = conserved[target].reshape(8, BLOCKS * 512).at[:, places.reshape(-1)].set(ordered, mode='drop')
        starts.append(target_flat.reshape(8, BLOCKS, 512))
    results = []
    for component in range(2):
        current = starts[component]
        for _ in range(STEPS):
            current = advance_all(current, ghost_rows_of(current, neighbours[component]), block_rate[component])
        results.append(current)
    return jnp.stack(results)
```

```python
import functools

import jax
import jax.numpy as jnp
from jax import lax
from jax.experimental import pallas as pl
from jax.experimental.pallas import tpu as pltpu
from jax.sharding import PartitionSpec as P

MESH = pl.DeviceIdType.MESH
STEPS = 3
REACH = 4
SLOTS = 32
GAMMA = 5.0 / 3.0
OFFSETS = list(range(-REACH, 0)) + list(range(1, REACH + 1))
SEND_ORDER = sorted(range(2 * REACH), key=lambda o: -abs(OFFSETS[o]))
F32, BF16, I32 = jnp.float32, jnp.bfloat16, jnp.int32


def primitives(u):
    inverse = 1.0 / u[0]
    v = [u[1] * inverse, u[2] * inverse, u[3] * inverse]
    kinetic = 0.5 * (u[1] * v[0] + u[2] * v[1] + u[3] * v[2])
    magnetic = 0.5 * (u[4] * u[4] + u[5] * u[5] + u[6] * u[6])
    pressure = (GAMMA - 1.0) * (u[7] - kinetic - magnetic)
    summed = pressure + magnetic
    align = v[0] * u[4] + v[1] * u[5] + v[2] * u[6]
    sound = GAMMA * pressure * inverse
    combined = sound + 2.0 * magnetic * inverse
    four = 4.0 * sound * inverse
    return v, summed, align, combined, four


def half_flux(u, prim, d):
    v, summed, align, combined, four = prim
    b = u[4:7]
    hn, hb = 0.5 * v[d], 0.5 * b[d]
    flux = [0.5 * u[1 + d]]
    for j in range(3):
        part = u[1 + j] * hn - b[j] * hb
        flux.append(part + 0.5 * summed if j == d else part)
    for j in range(3):
        flux.append(jnp.zeros_like(hn) if j == d else hn * b[j] - hb * v[j])
    flux.append((u[7] + summed) * hn - hb * align)
    inner = jnp.maximum(combined * combined - four * b[d] * b[d], 0.0)
    fast = jnp.sqrt(0.5 * (combined + jnp.sqrt(inner)))
    return flux, jnp.abs(hn) + 0.5 * fast


def take_lanes(table, index):
    rows = table.shape[0]
    return jnp.take_along_axis(
        table, jnp.broadcast_to(index, (rows, 128)), axis=1, mode="promise_in_bounds"
    )


def lane_iota(rows=1):
    return lax.broadcasted_iota(I32, (rows, 128), 1)


def kernel(
    nb, cons, rate, nbr, cell, frac, tgt, out,
    u, uhi, ulo, whi, wlo, tbuf, vbuf, msg, recv, oa, pbuf, acc,
    fs, hy, ft, gb, sb, hrecv, rt, idx,
    a_send, a_recv, h_send, h_recv,
):
    comp = lax.axis_index("comp")
    me = lax.axis_index("blk")
    lane = lane_iota()

    def exists(offset):
        return jnp.logical_and(me + offset >= 0, me + offset < nb)

    recv[...] = jnp.zeros_like(recv)
    rt[...] = jnp.zeros_like(rt)

    @pl.loop(0, STEPS)
    def _(s):
        hrecv[s] = jnp.zeros(hrecv.shape[1:], F32)

    barrier = pltpu.get_barrier_semaphore()

    @pl.loop(0, nb)
    def _(q):
        pl.semaphore_signal(barrier, inc=1, device_id=(1 - comp, q), device_id_type=MESH)

    for offset in OFFSETS:
        @pl.when(exists(offset))
        def _():
            pl.semaphore_signal(barrier, inc=1, device_id=(comp, me + offset), device_id_type=MESH)

    for var in range(8):
        for j in range(2):
            low = cons[var, :, 128 * j : 128 * j + 128]
            high = cons[var, :, 128 * j + 256 : 128 * j + 384]
            turned = jnp.concatenate([low, high], axis=0).T
            for k in range(2):
                part = turned[64 * k : 64 * k + 64]
                u[2 * j + k, var] = part
                upper = part.astype(BF16)
                at = (2 * j + k) * 128
                uhi[64 * var : 64 * var + 64, at : at + 128] = upper
                ulo[64 * var : 64 * var + 64, at : at + 128] = (part - upper.astype(F32)).astype(BF16)

    rows512 = lax.broadcasted_iota(I32, (512, 128), 0)
    sub8 = lax.broadcasted_iota(I32, (8, 128), 0)

    def interpolate(g):
        at = pl.multiple_of(g * 8, 8)
        cells = cell[pl.ds(at, 8), :]
        fxs, fys, fzs = (frac[k, pl.ds(at, 8), :] for k in range(3))
        x = (cells >> 6) & 7
        block = cells >> 9
        a0s = (x & 3) * 128 + (x >> 2) * 64 + block
        x1 = x + 1
        a1s = (x1 & 3) * 128 + (x1 >> 2) * 64 + block
        w0 = 1.0 - fxs
        w0h = w0.astype(BF16).astype(F32)
        w0l = w0 - w0h
        w1h = fxs.astype(BF16).astype(F32)
        w1l = fxs - w1h
        ys, zs = (cells >> 3) & 7, cells & 7
        for t in range(8):
            row = slice(t, t + 1)
            first = rows512 == a0s[row]
            second = rows512 == a1s[row]
            whi[:, 128 * t : 128 * t + 128] = jnp.where(
                first, w0h[row], jnp.where(second, w1h[row], 0.0)
            ).astype(BF16)
            wlo[:, 128 * t : 128 * t + 128] = jnp.where(
                first, w0l[row], jnp.where(second, w1l[row], 0.0)
            ).astype(BF16)
        tbuf[...] = (
            jnp.dot(uhi[...], whi[...], preferred_element_type=F32)
            + jnp.dot(ulo[...], whi[...], preferred_element_type=F32)
            + jnp.dot(uhi[...], wlo[...], preferred_element_type=F32)
        )
        for t in range(8):
            row = slice(t, t + 1)
            wz = jnp.where(sub8 == zs[row], 1.0 - fzs[row], jnp.where(sub8 == zs[row] + 1, fzs[row], 0.0))
            wys = []
            for y in range(8):
                wy = jnp.where(ys[row] == y, 1.0 - fys[row], jnp.where(ys[row] + 1 == y, fys[row], 0.0))
                wys.append(wy * wz)
            values = []
            for var in range(8):
                total = None
                for y in range(8):
                    term = wys[y] * tbuf[64 * var + 8 * y : 64 * var + 8 * y + 8, 128 * t : 128 * t + 128]
                    total = term if total is None else total + term
                values.append(jnp.sum(total, axis=0, keepdims=True))
            vbuf[pl.ds(pl.multiple_of(g * 64 + t * 8, 8), 8), :] = jnp.concatenate(values, axis=0)

    for half in range(2):
        @pl.loop(2 * half, 2 * half + 2)
        def _(g):
            interpolate(g)

        msg[half] = vbuf[128 * half : 128 * half + 128, :].T.reshape(128, 1, 128)
        if half == 0:
            near_by = jnp.minimum(me, REACH) + jnp.minimum(nb - 1 - me, REACH)
            pl.semaphore_wait(barrier, nb + near_by)

        @pl.loop(1, nb + 1)
        def _(i):
            q = lax.rem(me + i, nb)
            pltpu.make_async_remote_copy(
                src_ref=msg.at[half, q],
                dst_ref=recv.at[half, me],
                send_sem=a_send.at[half],
                recv_sem=a_recv.at[half],
                device_id=(1 - comp, q),
                device_id_type=MESH,
            ).start()

    targets = tgt[...]
    tx = (targets >> 6) & 7
    ta = jnp.where(
        targets < 64 * 512, (tx & 3) * 128 + (tx >> 2) * 64 + (targets >> 9), -1
    ).astype(F32)
    columns = jnp.concatenate([ta, jnp.zeros((96, 128), F32)], axis=0).T
    lanes512 = lax.broadcasted_iota(I32, (128, 512), 1).astype(F32)
    for s in range(SLOTS):
        oa[128 * s : 128 * s + 128, :] = jnp.where(
            lanes512 == columns[:, s : s + 1], 1.0, 0.0
        ).astype(BF16)

    links = nbr[...]
    links_c = jnp.concatenate([links.astype(F32), jnp.zeros((120, 128), F32)], axis=0).T.astype(I32)
    upper_lanes = lane >> 6
    half_lane = lane & 63
    group = (half_lane * 43) >> 8
    place = half_lane - 6 * group
    block_c = lax.broadcasted_iota(I32, (64, 1), 0)
    origin = {}
    for f in range(6):
        near = links[f : f + 1, :]
        far = links_c[0:64, f : f + 1]
        off_r = jnp.where(near >= 0, (near >> 6) - me, 0)
        off_c = jnp.where(far >= 0, (far >> 6) - me, 0)
        before = jnp.where((off_c == off_r) & ((far & 63) < (near & 63)), 1.0, 0.0)
        rank_r = jnp.sum(before, axis=0, keepdims=True).astype(I32)
        earlier = jnp.where((off_c == off_r) & (lane < block_c), 1.0, 0.0)
        rank_c = jnp.sum(earlier, axis=1, keepdims=True).astype(I32)
        slot_c = jnp.where(off_c < 0, off_c + REACH, off_c + REACH - 1)
        slot_c = jnp.where(off_c == 0, -1, slot_c)
        slot_r = jnp.where(off_r < 0, off_r + REACH, off_r + REACH - 1)
        if f < 2:
            wanted = jnp.where(place >= 3, place - 3, place)
            mine = (place >= 3) if f == 1 else (place < 3)
        else:
            wanted = place >> 1
            mine = place >= 0
        hit = (slot_c == group) & (rank_c == wanted) & mine
        which = jnp.sum(jnp.where(hit, block_c.astype(F32), 0.0), axis=0, keepdims=True).astype(I32)
        origin[f] = (off_r, near, rank_r, slot_r, which)
    side = upper_lanes

    def pick(a, b):
        return jnp.where(side == 0, a, b)

    idx[0:1, :] = jnp.where(place >= 3, 64 + origin[1][4], origin[0][4])
    off_x = pick(origin[0][0], origin[1][0])
    near_x = pick(origin[0][1], origin[1][1])
    rank_x = pick(origin[0][2], origin[1][2])
    slot_x = pick(origin[0][3], origin[1][3])
    idx[3:4, :] = jnp.where(near_x >= 0, (1 - side) * 64 + (near_x & 63), lane)
    idx[4:5, :] = jnp.where(off_x != 0, slot_x * 6 + (1 - side) * 3 + rank_x, -1)
    for d in (1, 2):
        idx[d : d + 1, :] = 64 * (place & 1) + pick(origin[2 * d][4], origin[2 * d + 1][4])
        for high in range(2):
            off, near, rank, slot, _ = origin[2 * d + high]
            at = 5 + 6 * (d - 1) + 3 * high
            idx[at : at + 1, :] = jnp.where(near >= 0, 64 * side + (near & 63), -1)
            idx[at + 1 : at + 2, :] = jnp.where(
                off != 0, slot * 6 + rank * 2 + side + (0 if high else 64), -1
            )

    rows64 = lax.broadcasted_iota(I32, (64, 128), 0)
    for half in range(2):
        whole = recv.at[half, pl.ds(0, nb)]
        pltpu.make_async_copy(whole, whole, a_recv.at[half]).wait()
        vbuf[128 * half : 128 * half + 128, :] = recv[half].reshape(128, 128).T
    acc[...] = jnp.zeros_like(acc)

    @pl.loop(0, 4)
    def _(g):
        places = tgt[pl.ds(pl.multiple_of(g * 8, 8), 8), :] & 63
        for t in range(8):
            value = vbuf[pl.ds(pl.multiple_of(g * 64 + t * 8, 8), 8), :]
            upper = value.astype(BF16).astype(F32)
            lower = value - upper
            here = rows64 == places[t : t + 1]
            cols = slice(128 * t, 128 * t + 128)
            for var in range(8):
                pbuf[64 * var : 64 * var + 64, cols] = jnp.where(here, upper[var : var + 1], 0.0).astype(BF16)
                pbuf[512 + 64 * var : 576 + 64 * var, cols] = jnp.where(here, lower[var : var + 1], 0.0).astype(BF16)
            pbuf[1024:1088, cols] = jnp.where(here, 1.0, 0.0).astype(BF16)
        acc[...] += jnp.dot(
            pbuf[...], oa[pl.ds(pl.multiple_of(g * 1024, 1024), 1024), :], preferred_element_type=F32
        )

    for xl in range(4):
        cols = slice(128 * xl, 128 * xl + 128)
        changed = acc[1024:1088, cols] > 0.5
        for var in range(8):
            rows = slice(64 * var, 64 * var + 64)
            lower = slice(512 + 64 * var, 576 + 64 * var)
            u[xl, var] = jnp.where(changed, acc[rows, cols] + acc[lower, cols], u[xl, var])
    for half in range(2):
        whole = msg.at[half, pl.ds(0, nb)]
        pltpu.make_async_copy(whole, whole, a_send.at[half]).wait()

    rates = rate[...]
    low_lanes = lane_iota(8) < 64
    swap = functools.partial(pltpu.roll, shift=64, axis=1)

    def copy_of(step, pair, o):
        offset = OFFSETS[o]
        return pltpu.make_async_remote_copy(
            src_ref=sb.at[pair, o],
            dst_ref=hrecv.at[step, pair, OFFSETS.index(-offset)],
            send_sem=h_send.at[step, pair, o],
            recv_sem=h_recv.at[step, pair, OFFSETS.index(-offset)],
            device_id=(comp, me + offset),
            device_id_type=MESH,
        )

    def tile(y):
        return pl.ds(pl.multiple_of(y * 8, 8), 8)

    @pl.loop(0, STEPS)
    def _(step):
        for pair in range(3):
            for xl in range(4):
                for var in range(8):
                    at = slice(64 * xl + 8 * var, 64 * xl + 8 * var + 8)
                    if pair == 1:
                        ft[2, at, :] = u[xl, var, 0:8, :]
                        ft[3, at, :] = u[xl, var, 56:64, :]
                    elif pair == 2:
                        ft[4, at, :] = u[xl, var, pl.ds(0, 8, stride=8), :]
                        ft[5, at, :] = u[xl, var, pl.ds(7, 8, stride=8), :]
            if pair == 0:
                for var in range(8):
                    ft[var // 4, 64 * (var % 4) : 64 * (var % 4) + 64, :] = jnp.where(
                        lane < 64, u[0, var], u[3, var]
                    )
            take = idx[pair : pair + 1, :]
            packed = jnp.where(lane < 64, take_lanes(ft[2 * pair], take), take_lanes(ft[2 * pair + 1], take))
            for r in range(2):
                turned = packed[128 * r : 128 * r + 128].T
                for o in range(8):
                    for s in range(2):
                        sb[pair, o, 12 * s + 6 * r : 12 * s + 6 * r + 6, :] = turned[
                            64 * s + 6 * o : 64 * s + 6 * o + 6
                        ]
            for o in SEND_ORDER:
                @pl.when(exists(OFFSETS[o]))
                def _():
                    copy_of(step, pair, o).start()

        @pl.loop(0, 8)
        def _(y):
            for xl in range(4):
                cells = [u[xl, var, tile(y), :] for var in range(8)]
                prim = primitives(cells)
                for d in range(3):
                    flux, speed = half_flux(cells, prim, d)
                    for c in range(8):
                        fs[d, xl, c, tile(y), :] = flux[c]
                    fs[d, xl, 8, tile(y), :] = speed

        hy[...] = jnp.zeros_like(hy)

        @pl.loop(0, 8)
        def _(y):
            here, above = tile(y), tile(jnp.minimum(y + 1, 7))
            keep_y = jnp.where(y < 7, 1.0, 0.0)
            keep_z = sub8 < 7
            sx = [fs[0, xl, 8, here, :] for xl in range(4)]
            mx = [jnp.maximum(sx[xl], sx[xl + 1]) for xl in range(3)]
            mx.append(jnp.maximum(sx[3], swap(sx[0])))
            my, mz = [], []
            for xl in range(4):
                my.append(jnp.maximum(fs[1, xl, 8, here, :], fs[1, xl, 8, above, :]))
                sz = fs[2, xl, 8, here, :]
                mz.append(jnp.maximum(sz, pltpu.roll(sz, 7, 0)))
            for c in range(8):
                state = [u[xl, c, here, :] for xl in range(4)]
                fx = [fs[0, xl, c, here, :] for xl in range(4)]
                hx = []
                for xl in range(3):
                    hx.append(fx[xl] + fx[xl + 1] - mx[xl] * (state[xl + 1] - state[xl]))
                last = fx[3] + swap(fx[0]) - mx[3] * (swap(state[0]) - state[3])
                hx.append(jnp.where(low_lanes, last, 0.0))
                for xl in range(4):
                    change = hx[xl] - (hx[xl - 1] if xl else swap(hx[3]))
                    up = (
                        fs[1, xl, c, here, :] + fs[1, xl, c, above, :]
                        - my[xl] * (u[xl, c, above, :] - state[xl])
                    ) * keep_y
                    change = change + (up - hy[xl, c])
                    hy[xl, c] = up
                    fz = fs[2, xl, c, here, :]
                    right = fz + pltpu.roll(fz, 7, 0) - mz[xl] * (pltpu.roll(state[xl], 7, 0) - state[xl])
                    right = jnp.where(keep_z, right, 0.0)
                    change = change + (right - pltpu.roll(right, 1, 0))
                    u[xl, c, here, :] = state[xl] - rates * change

        def edge(own, ghost, d, sign):
            own_flux, own_speed = half_flux(own, primitives(own), d)
            far_flux, far_speed = half_flux(ghost, primitives(ghost), d)
            most = jnp.maximum(own_speed, far_speed)
            return [
                rates * (sign * (own_flux[c] + far_flux[c]) - most * (own[c] - ghost[c]))
                for c in range(8)
            ]

        for pair in range(3):
            for o in range(8):
                @pl.when(exists(-OFFSETS[o]))
                def _():
                    copy_of(step, pair, o).wait_recv()
            for o in range(8):
                for r in range(2):
                    for s in range(2):
                        rt[r, 64 * s + 6 * o : 64 * s + 6 * o + 6, :] = hrecv[
                            step, pair, o, 12 * s + 6 * r : 12 * s + 6 * r + 6, :
                        ]
            arrived = jnp.concatenate([rt[0].T, rt[1].T], axis=0)
            if pair == 0:
                near = idx[3:4, :]
                far = idx[4:5, :]
                for s in range(2):
                    gb[s] = jnp.where(
                        far >= 0,
                        take_lanes(arrived, jnp.maximum(far, 0) + 64 * s),
                        take_lanes(ft[s], near),
                    )

                @pl.loop(0, 8)
                def _(y):
                    own = [ft[c // 4, pl.ds(pl.multiple_of(64 * (c % 4) + y * 8, 8), 8), :] for c in range(8)]
                    ghost = [gb[c // 4, pl.ds(pl.multiple_of(64 * (c % 4) + y * 8, 8), 8), :] for c in range(8)]
                    delta = edge(own, ghost, 0, jnp.where(low_lanes, 1.0, -1.0))
                    for c in range(8):
                        u[0, c, tile(y), :] = u[0, c, tile(y), :] + jnp.where(low_lanes, delta[c], 0.0)
                        u[3, c, tile(y), :] = u[3, c, tile(y), :] + jnp.where(low_lanes, 0.0, delta[c])
            else:
                for high in range(2):
                    at = 5 + 6 * (pair - 1) + 3 * high
                    near = idx[at : at + 1, :]
                    far = idx[at + 1 : at + 2, :]
                    local = jnp.where(
                        near >= 0,
                        take_lanes(ft[2 * pair + 1 - high], jnp.maximum(near, 0)),
                        ft[2 * pair + high],
                    )
                    gb[high] = jnp.where(far >= 0, take_lanes(arrived, jnp.maximum(far, 0)), local)
                    for xl in range(4):
                        rows = [slice(64 * xl + 8 * c, 64 * xl + 8 * c + 8) for c in range(8)]
                        own = [ft[2 * pair + high, rows[c], :] for c in range(8)]
                        ghost = [gb[high, rows[c], :] for c in range(8)]
                        delta = edge(own, ghost, pair, -1.0 if high else 1.0)
                        for c in range(8):
                            if pair == 1:
                                part = slice(56, 64) if high else slice(0, 8)
                            else:
                                part = pl.ds(7 if high else 0, 8, stride=8)
                            u[xl, c, part, :] = u[xl, c, part, :] + delta[c]

        for pair in range(3):
            for o in range(8):
                @pl.when(exists(OFFSETS[o]))
                def _():
                    copy_of(step, pair, o).wait_send()

    for var in range(8):
        for j in range(2):
            turned = jnp.concatenate([u[2 * j, var], u[2 * j + 1, var]], axis=0).T
            out[var, :, 128 * j : 128 * j + 128] = turned[0:64]
            out[var, :, 128 * j + 256 : 128 * j + 384] = turned[64:128]


def on_device(nb, conserved, block_rate, neighbours, shell_cell, shell_frac, shell_target):
    extra = 128 - nb
    cell = jnp.pad(shell_cell[0, 0].T, ((0, 0), (0, extra)))
    frac = jnp.pad(shell_frac[0, :, 0].transpose(0, 2, 1), ((0, 0), (0, 0), (0, extra)))
    target = jnp.pad(shell_target[0, 0].T, ((0, 0), (0, extra)), constant_values=64 * 512)
    links = neighbours[0].T
    links = jnp.pad(jnp.concatenate([links, links], axis=1), ((0, 2), (0, 0)), constant_values=-1)
    rates = jnp.concatenate([block_rate, block_rate], axis=1)
    vmem = pl.BlockSpec(memory_space=pltpu.VMEM)
    result = pl.pallas_call(
        functools.partial(kernel, nb),
        out_shape=jax.ShapeDtypeStruct((8, 64, 512), F32),
        in_specs=[vmem] * 6,
        out_specs=vmem,
        scratch_shapes=[
            pltpu.VMEM((4, 8, 64, 128), F32),
            pltpu.VMEM((512, 512), BF16),
            pltpu.VMEM((512, 512), BF16),
            pltpu.VMEM((512, 1024), BF16),
            pltpu.VMEM((512, 1024), BF16),
            pltpu.VMEM((512, 1024), F32),
            pltpu.VMEM((256, 128), F32),
            pltpu.VMEM((2, 128, 1, 128), F32),
            pltpu.VMEM((2, 128, 1, 128), F32),
            pltpu.VMEM((4096, 512), BF16),
            pltpu.VMEM((1088, 1024), BF16),
            pltpu.VMEM((1088, 512), F32),
            pltpu.VMEM((3, 4, 9, 64, 128), F32),
            pltpu.VMEM((4, 8, 8, 128), F32),
            pltpu.VMEM((6, 256, 128), F32),
            pltpu.VMEM((2, 256, 128), F32),
            pltpu.VMEM((3, 8, 24, 128), F32),
            pltpu.VMEM((STEPS, 3, 8, 24, 128), F32),
            pltpu.VMEM((2, 128, 128), F32),
            pltpu.VMEM((24, 128), I32),
            pltpu.SemaphoreType.DMA((2,)),
            pltpu.SemaphoreType.DMA((2,)),
            pltpu.SemaphoreType.DMA((STEPS, 3, 8)),
            pltpu.SemaphoreType.DMA((STEPS, 3, 8)),
        ],
        compiler_params=pltpu.CompilerParams(
            collective_id=0, has_side_effects=True, vmem_limit_bytes=48 << 20
        ),
    )(conserved[0], rates, links, cell, frac, target)
    return result[None]


def solution(mesh):
    return jax.shard_map(
        functools.partial(on_device, mesh.shape["blk"]),
        mesh=mesh,
        in_specs=(
            P("comp", None, "blk", None),
            P("comp", "blk"),
            P("comp", "blk", None),
            P("comp", "blk", None, None),
            P("comp", None, "blk", None, None),
            P("comp", "blk", None, None),
        ),
        out_specs=P("comp", None, "blk", None),
        check_vma=False,
    )
```

```python
import functools

import jax
import jax.numpy as jnp
from jax import lax
from jax.experimental import pallas as pl
from jax.experimental.pallas import tpu as pltpu
from jax.sharding import PartitionSpec as P

MESH = pl.DeviceIdType.MESH
STEPS = 3
REACH = 4
SLOTS = 32
GAMMA = 5.0 / 3.0
OFFSETS = list(range(-REACH, 0)) + list(range(1, REACH + 1))
SEND_ORDER = sorted(range(2 * REACH), key=lambda o: -abs(OFFSETS[o]))
F32, BF16, I32 = jnp.float32, jnp.bfloat16, jnp.int32


def primitives(u):
    inverse = 1.0 / u[0]
    v = [u[1] * inverse, u[2] * inverse, u[3] * inverse]
    kinetic = 0.5 * (u[1] * v[0] + u[2] * v[1] + u[3] * v[2])
    magnetic = 0.5 * (u[4] * u[4] + u[5] * u[5] + u[6] * u[6])
    pressure = (GAMMA - 1.0) * (u[7] - kinetic - magnetic)
    summed = pressure + magnetic
    align = v[0] * u[4] + v[1] * u[5] + v[2] * u[6]
    sound = GAMMA * pressure * inverse
    combined = sound + 2.0 * magnetic * inverse
    four = 4.0 * sound * inverse
    return v, summed, align, combined, four


def half_flux(u, prim, d):
    v, summed, align, combined, four = prim
    b = u[4:7]
    hn, hb = 0.5 * v[d], 0.5 * b[d]
    flux = [0.5 * u[1 + d]]
    for j in range(3):
        part = u[1 + j] * hn - b[j] * hb
        flux.append(part + 0.5 * summed if j == d else part)
    for j in range(3):
        flux.append(jnp.zeros_like(hn) if j == d else hn * b[j] - hb * v[j])
    flux.append((u[7] + summed) * hn - hb * align)
    inner = jnp.maximum(combined * combined - four * b[d] * b[d], 0.0)
    fast = jnp.sqrt(0.5 * (combined + jnp.sqrt(inner)))
    return flux, jnp.abs(hn) + 0.5 * fast


def take_lanes(table, index):
    rows = table.shape[0]
    return jnp.take_along_axis(
        table, jnp.broadcast_to(index, (rows, 128)), axis=1, mode="promise_in_bounds"
    )


def lane_iota(rows=1):
    return lax.broadcasted_iota(I32, (rows, 128), 1)


def kernel(
    nb, cons_hbm, rate_hbm, nbr_hbm, cell_hbm, frac_hbm, tgt_hbm, out,
    cons, rate, nbr, cell, frac, tgt, links, in_sem,
    cur, ub, wb, tbuf, vbuf, msg, recv, oa, pbuf, acc,
    fs, hy, old, ft, gb, sb, hrecv, rt, idx,
    a_send, a_recv, h_send, h_recv,
):
    comp = lax.axis_index("comp")
    me = lax.axis_index("blk")
    lane = lane_iota()

    def exists(offset):
        return jnp.logical_and(me + offset >= 0, me + offset < nb)

    loads = [
        pltpu.make_async_copy(source, held, in_sem.at[k])
        for k, (source, held) in enumerate(
            ((cell_hbm, cell), (frac_hbm, frac), (cons_hbm, cons), (tgt_hbm, tgt), (nbr_hbm, nbr), (rate_hbm, rate))
        )
    ]
    for load in loads:
        load.start()

    if nb < 128:
        recv[...] = jnp.zeros_like(recv)
    rt[...] = jnp.zeros_like(rt)

    @pl.loop(0, STEPS)
    def _(s):
        hrecv[s] = jnp.zeros(hrecv.shape[1:], F32)

    barrier = pltpu.get_barrier_semaphore()

    @pl.loop(0, nb)
    def _(q):
        pl.semaphore_signal(barrier, inc=1, device_id=(1 - comp, q), device_id_type=MESH)

    for offset in OFFSETS:
        @pl.when(exists(offset))
        def _():
            pl.semaphore_signal(barrier, inc=1, device_id=(comp, me + offset), device_id_type=MESH)

    for load in loads:
        load.wait()
    for var in range(8):
        for j in range(2):
            low = cons[var, :, 128 * j : 128 * j + 128]
            high = cons[var, :, 128 * j + 256 : 128 * j + 384]
            turned = jnp.concatenate([low, high], axis=0).T
            for k in range(2):
                part = turned[64 * k : 64 * k + 64]
                cur[2 * j + k, var] = part
                upper = part.astype(BF16)
                at = (2 * j + k) * 128
                rows = slice(64 * var, 64 * var + 64)
                ub[rows, at : at + 128] = upper
                ub[rows, at + 512 : at + 640] = (part - upper.astype(F32)).astype(BF16)
                ub[rows, at + 1024 : at + 1152] = upper

    def send_values(half):
        def send(q):
            pltpu.make_async_remote_copy(
                src_ref=msg.at[half, q],
                dst_ref=recv.at[half, me],
                send_sem=a_send.at[half],
                recv_sem=a_recv.at[half],
                device_id=(1 - comp, q),
                device_id_type=MESH,
            ).start()

        if nb == 128:
            planes = [
                lax.rem(me // 32 + dx, 4) * 32 + lax.rem(me // 8 + dy, 4) * 8
                for dx, dy in ((2, 2), (2, 1), (2, 3), (1, 2), (3, 2), (1, 1), (1, 3), (3, 1), (3, 3),
                               (2, 0), (0, 2), (1, 0), (3, 0), (0, 1), (0, 3), (0, 0))
            ]
            height = lax.rem(me, 8)

            @pl.loop(0, 8)
            def _(j):
                step = (j + 1) // 2
                z = lax.rem(height + 4 + step * (1 - 2 * lax.rem(j, 2)), 8)
                for plane in planes:
                    send(plane + z)
        else:
            @pl.loop(1, nb + 1)
            def _(i):
                send(lax.rem(me + i, nb))

    rows64 = lax.broadcasted_iota(I32, (64, 128), 0)
    sub8 = lax.broadcasted_iota(I32, (8, 128), 0)

    def interpolate(g):
        at = pl.multiple_of(g * 8, 8)
        cells = cell[pl.ds(at, 8), :]
        fxs, fys, fzs = (frac[k, pl.ds(at, 8), :] for k in range(3))
        xs = (cells >> 6) & 7
        blocks = cells >> 9
        ys, zs = (cells >> 3) & 7, cells & 7

        def along(corners, fractions, row):
            first, part = corners[row], fractions[row]
            return jnp.where(sub8 == first, 1.0 - part, jnp.where(sub8 == first + 1, part, 0.0))

        for t in range(8):
            row = slice(t, t + 1)
            cols = slice(128 * t, 128 * t + 128)
            wx = along(xs, fxs, row)
            upper = wx.astype(BF16).astype(F32)
            lower = wx - upper
            inside = rows64 == blocks[row]
            for x in range(8):
                at = (x & 3) * 128 + (x >> 2) * 64
                part = jnp.where(inside, upper[x : x + 1], 0.0).astype(BF16)
                wb[at : at + 64, cols] = part
                wb[at + 512 : at + 576, cols] = part
                wb[at + 1024 : at + 1088, cols] = jnp.where(inside, lower[x : x + 1], 0.0).astype(BF16)
        tbuf[...] = jnp.dot(ub[...], wb[...], preferred_element_type=F32)
        for t in range(8):
            row = slice(t, t + 1)
            wz = along(zs, fzs, row)
            wy = along(ys, fys, row)
            wys = [wy[y : y + 1] * wz for y in range(8)]
            values = []
            for var in range(8):
                total = None
                for y in range(8):
                    term = wys[y] * tbuf[64 * var + 8 * y : 64 * var + 8 * y + 8, 128 * t : 128 * t + 128]
                    total = term if total is None else total + term
                values.append(jnp.sum(total, axis=0, keepdims=True))
            vbuf[pl.ds(pl.multiple_of(g * 64 + t * 8, 8), 8), :] = jnp.concatenate(values, axis=0)

    for half in range(2):
        @pl.loop(2 * half, 2 * half + 2)
        def _(g):
            interpolate(g)

        msg[half] = vbuf[128 * half : 128 * half + 128, :].T.reshape(128, 1, 128)
        if half == 0:
            near_by = jnp.minimum(me, REACH) + jnp.minimum(nb - 1 - me, REACH)
            pl.semaphore_wait(barrier, nb + near_by)

        send_values(half)

    targets = tgt[...]
    tx = (targets >> 6) & 7
    ta = jnp.where(
        targets < 64 * 512, (tx & 3) * 128 + (tx >> 2) * 64 + (targets >> 9), -1
    ).astype(F32)
    columns = jnp.concatenate([ta, jnp.zeros((96, 128), F32)], axis=0).T
    lanes512 = lax.broadcasted_iota(I32, (128, 512), 1).astype(F32)
    for s in range(SLOTS):
        oa[128 * s : 128 * s + 128, :] = jnp.where(
            lanes512 == columns[:, s : s + 1], 1.0, 0.0
        ).astype(BF16)

    links[...] = jnp.full_like(links, -1)
    for f in range(6):
        links[f : f + 1, 0:64] = nbr[f]
        links[f : f + 1, 64:128] = nbr[f]
    links_c = jnp.concatenate([links[...].astype(F32), jnp.zeros((120, 128), F32)], axis=0).T.astype(I32)
    upper_lanes = lane >> 6
    half_lane = lane & 63
    group = (half_lane * 43) >> 8
    place = half_lane - 6 * group
    block_c = lax.broadcasted_iota(I32, (64, 1), 0)
    origin = {}
    for f in range(6):
        near = links[f : f + 1, :]
        far = links_c[0:64, f : f + 1]
        off_r = jnp.where(near >= 0, (near >> 6) - me, 0)
        off_c = jnp.where(far >= 0, (far >> 6) - me, 0)
        before = jnp.where((off_c == off_r) & ((far & 63) < (near & 63)), 1.0, 0.0)
        rank_r = jnp.sum(before, axis=0, keepdims=True).astype(I32)
        earlier = jnp.where((off_c == off_r) & (lane < block_c), 1.0, 0.0)
        rank_c = jnp.sum(earlier, axis=1, keepdims=True).astype(I32)
        slot_c = jnp.where(off_c < 0, off_c + REACH, off_c + REACH - 1)
        slot_c = jnp.where(off_c == 0, -1, slot_c)
        slot_r = jnp.where(off_r < 0, off_r + REACH, off_r + REACH - 1)
        if f < 2:
            wanted = jnp.where(place >= 3, place - 3, place)
            mine = (place >= 3) if f == 1 else (place < 3)
        else:
            wanted = place >> 1
            mine = place >= 0
        hit = (slot_c == group) & (rank_c == wanted) & mine
        which = jnp.sum(jnp.where(hit, block_c.astype(F32), 0.0), axis=0, keepdims=True).astype(I32)
        origin[f] = (off_r, near, rank_r, slot_r, which)
    side = upper_lanes

    def pick(a, b):
        return jnp.where(side == 0, a, b)

    idx[0:1, :] = jnp.where(place >= 3, 64 + origin[1][4], origin[0][4])
    off_x = pick(origin[0][0], origin[1][0])
    near_x = pick(origin[0][1], origin[1][1])
    rank_x = pick(origin[0][2], origin[1][2])
    slot_x = pick(origin[0][3], origin[1][3])
    idx[3:4, :] = jnp.where(near_x >= 0, (1 - side) * 64 + (near_x & 63), lane)
    idx[4:5, :] = jnp.where(off_x != 0, slot_x * 6 + (1 - side) * 3 + rank_x, -1)
    for d in (1, 2):
        idx[d : d + 1, :] = 64 * (place & 1) + pick(origin[2 * d][4], origin[2 * d + 1][4])
        for high in range(2):
            off, near, rank, slot, _ = origin[2 * d + high]
            at = 5 + 6 * (d - 1) + 3 * high
            idx[at : at + 1, :] = jnp.where(near >= 0, 64 * side + (near & 63), -1)
            idx[at + 1 : at + 2, :] = jnp.where(
                off != 0, slot * 6 + rank * 2 + side + (0 if high else 64), -1
            )

    acc[...] = jnp.zeros_like(acc)
    for half in range(2):
        whole = recv.at[half, pl.ds(0, nb)]
        pltpu.make_async_copy(whole, whole, a_recv.at[half]).wait()
        vbuf[128 * half : 128 * half + 128, :] = recv[half].reshape(128, 128).T

        @pl.loop(2 * half, 2 * half + 2)
        def _(g):
            places = tgt[pl.ds(pl.multiple_of(g * 8, 8), 8), :] & 63
            for t in range(8):
                value = vbuf[pl.ds(pl.multiple_of(g * 64 + t * 8, 8), 8), :]
                upper = value.astype(BF16).astype(F32)
                lower = value - upper
                here = rows64 == places[t : t + 1]
                cols = slice(128 * t, 128 * t + 128)
                for var in range(8):
                    pbuf[64 * var : 64 * var + 64, cols] = jnp.where(here, upper[var : var + 1], 0.0).astype(BF16)
                    pbuf[512 + 64 * var : 576 + 64 * var, cols] = jnp.where(here, lower[var : var + 1], 0.0).astype(BF16)
                pbuf[1024:1088, cols] = jnp.where(here, 1.0, 0.0).astype(BF16)
            acc[...] += jnp.dot(
                pbuf[...], oa[pl.ds(pl.multiple_of(g * 1024, 1024), 1024), :], preferred_element_type=F32
            )

    for xl in range(4):
        cols = slice(128 * xl, 128 * xl + 128)
        changed = acc[1024:1088, cols] > 0.5
        for var in range(8):
            rows = slice(64 * var, 64 * var + 64)
            lower = slice(512 + 64 * var, 576 + 64 * var)
            cur[xl, var] = jnp.where(changed, acc[rows, cols] + acc[lower, cols], cur[xl, var])
    for half in range(2):
        whole = msg.at[half, pl.ds(0, nb)]
        pltpu.make_async_copy(whole, whole, a_send.at[half]).wait()

    rates = jnp.concatenate([rate[...], rate[...]], axis=1)
    low_lanes = lane_iota(8) < 64
    swap = functools.partial(pltpu.roll, shift=64, axis=1)

    def copy_of(step, pair, o):
        offset = OFFSETS[o]
        return pltpu.make_async_remote_copy(
            src_ref=sb.at[pair, o],
            dst_ref=hrecv.at[step, pair, OFFSETS.index(-offset)],
            send_sem=h_send.at[step, pair, o],
            recv_sem=h_recv.at[step, pair, OFFSETS.index(-offset)],
            device_id=(comp, me + offset),
            device_id_type=MESH,
        )

    def tile(y):
        return pl.ds(pl.multiple_of(y * 8, 8), 8)

    @pl.loop(0, STEPS)
    def _(step):
        for pair in range(3):
            for xl in range(4):
                for var in range(8):
                    at = slice(64 * xl + 8 * var, 64 * xl + 8 * var + 8)
                    if pair == 1:
                        ft[2, at, :] = cur[xl, var, 0:8, :]
                        ft[3, at, :] = cur[xl, var, 56:64, :]
                    elif pair == 2:
                        ft[4, at, :] = cur[xl, var, pl.ds(0, 8, stride=8), :]
                        ft[5, at, :] = cur[xl, var, pl.ds(7, 8, stride=8), :]
            if pair == 0:
                for var in range(8):
                    ft[var // 4, 64 * (var % 4) : 64 * (var % 4) + 64, :] = jnp.where(
                        lane < 64, cur[0, var], cur[3, var]
                    )
            take = idx[pair : pair + 1, :]
            packed = jnp.where(lane < 64, take_lanes(ft[2 * pair], take), take_lanes(ft[2 * pair + 1], take))
            for r in range(2):
                turned = packed[128 * r : 128 * r + 128].T
                for o in range(8):
                    for s in range(2):
                        sb[pair, o, 12 * s + 6 * r : 12 * s + 6 * r + 6, :] = turned[
                            64 * s + 6 * o : 64 * s + 6 * o + 6
                        ]
            for o in SEND_ORDER:
                @pl.when(exists(OFFSETS[o]))
                def _():
                    copy_of(step, pair, o).start()

        @pl.loop(0, 8)
        def _(y):
            for xl in range(4):
                cells = [cur[xl, var, tile(y), :] for var in range(8)]
                for var in range(8):
                    old[xl, var, tile(y), :] = cells[var]
                prim = primitives(cells)
                for d in range(3):
                    flux, speed = half_flux(cells, prim, d)
                    for c in range(8):
                        fs[d, xl, c, tile(y), :] = flux[c]
                    fs[d, xl, 8, tile(y), :] = speed

        hy[...] = jnp.zeros_like(hy)

        @pl.loop(0, 8)
        def _(y):
            here, above = tile(y), tile(jnp.minimum(y + 1, 7))
            keep_y = jnp.where(y < 7, 1.0, 0.0)
            keep_z = sub8 < 7
            sx = [fs[0, xl, 8, here, :] for xl in range(4)]
            mx = [jnp.maximum(sx[xl], sx[xl + 1]) for xl in range(3)]
            mx.append(jnp.maximum(sx[3], swap(sx[0])))
            my, mz = [], []
            for xl in range(4):
                my.append(jnp.maximum(fs[1, xl, 8, here, :], fs[1, xl, 8, above, :]))
                sz = fs[2, xl, 8, here, :]
                mz.append(jnp.maximum(sz, pltpu.roll(sz, 7, 0)))
            for c in range(8):
                state = [old[xl, c, here, :] for xl in range(4)]
                fx = [fs[0, xl, c, here, :] for xl in range(4)]
                hx = []
                for xl in range(3):
                    hx.append(fx[xl] + fx[xl + 1] - mx[xl] * (state[xl + 1] - state[xl]))
                last = fx[3] + swap(fx[0]) - mx[3] * (swap(state[0]) - state[3])
                hx.append(jnp.where(low_lanes, last, 0.0))
                for xl in range(4):
                    change = hx[xl] - (hx[xl - 1] if xl else swap(hx[3]))
                    up = (
                        fs[1, xl, c, here, :] + fs[1, xl, c, above, :]
                        - my[xl] * (old[xl, c, above, :] - state[xl])
                    ) * keep_y
                    change = change + (up - hy[xl, c])
                    hy[xl, c] = up
                    fz = fs[2, xl, c, here, :]
                    right = fz + pltpu.roll(fz, 7, 0) - mz[xl] * (pltpu.roll(state[xl], 7, 0) - state[xl])
                    right = jnp.where(keep_z, right, 0.0)
                    change = change + (right - pltpu.roll(right, 1, 0))
                    cur[xl, c, here, :] = state[xl] - rates * change

        def edge(own, ghost, d, sign):
            own_flux, own_speed = half_flux(own, primitives(own), d)
            far_flux, far_speed = half_flux(ghost, primitives(ghost), d)
            most = jnp.maximum(own_speed, far_speed)
            return [
                rates * (sign * (own_flux[c] + far_flux[c]) - most * (own[c] - ghost[c]))
                for c in range(8)
            ]

        for pair in range(3):
            for o in range(8):
                @pl.when(exists(-OFFSETS[o]))
                def _():
                    copy_of(step, pair, o).wait_recv()
            for o in range(8):
                for r in range(2):
                    for s in range(2):
                        rt[r, 64 * s + 6 * o : 64 * s + 6 * o + 6, :] = hrecv[
                            step, pair, o, 12 * s + 6 * r : 12 * s + 6 * r + 6, :
                        ]
            arrived = jnp.concatenate([rt[0].T, rt[1].T], axis=0)
            if pair == 0:
                near = idx[3:4, :]
                far = idx[4:5, :]
                for s in range(2):
                    gb[s] = jnp.where(
                        far >= 0,
                        take_lanes(arrived, jnp.maximum(far, 0) + 64 * s),
                        take_lanes(ft[s], near),
                    )

                @pl.loop(0, 8)
                def _(y):
                    own = [ft[c // 4, pl.ds(pl.multiple_of(64 * (c % 4) + y * 8, 8), 8), :] for c in range(8)]
                    ghost = [gb[c // 4, pl.ds(pl.multiple_of(64 * (c % 4) + y * 8, 8), 8), :] for c in range(8)]
                    delta = edge(own, ghost, 0, jnp.where(low_lanes, 1.0, -1.0))
                    for c in range(8):
                        cur[0, c, tile(y), :] = cur[0, c, tile(y), :] + jnp.where(low_lanes, delta[c], 0.0)
                        cur[3, c, tile(y), :] = cur[3, c, tile(y), :] + jnp.where(low_lanes, 0.0, delta[c])
            else:
                for high in range(2):
                    at = 5 + 6 * (pair - 1) + 3 * high
                    near = idx[at : at + 1, :]
                    far = idx[at + 1 : at + 2, :]
                    local = jnp.where(
                        near >= 0,
                        take_lanes(ft[2 * pair + 1 - high], jnp.maximum(near, 0)),
                        ft[2 * pair + high],
                    )
                    gb[high] = jnp.where(far >= 0, take_lanes(arrived, jnp.maximum(far, 0)), local)
                    for xl in range(4):
                        rows = [slice(64 * xl + 8 * c, 64 * xl + 8 * c + 8) for c in range(8)]
                        own = [ft[2 * pair + high, rows[c], :] for c in range(8)]
                        ghost = [gb[high, rows[c], :] for c in range(8)]
                        delta = edge(own, ghost, pair, -1.0 if high else 1.0)
                        for c in range(8):
                            if pair == 1:
                                part = slice(56, 64) if high else slice(0, 8)
                            else:
                                part = pl.ds(7 if high else 0, 8, stride=8)
                            cur[xl, c, part, :] = cur[xl, c, part, :] + delta[c]

        for pair in range(3):
            for o in range(8):
                @pl.when(exists(OFFSETS[o]))
                def _():
                    copy_of(step, pair, o).wait_send()

    for var in range(8):
        for j in range(2):
            turned = jnp.concatenate([cur[2 * j, var], cur[2 * j + 1, var]], axis=0).T
            out[var, :, 128 * j : 128 * j + 128] = turned[0:64]
            out[var, :, 128 * j + 256 : 128 * j + 384] = turned[64:128]


def on_device(nb, conserved, block_rate, neighbours, shell_cell, shell_frac, shell_target):
    extra = 128 - nb
    cell = jnp.pad(shell_cell[0, 0].T, ((0, 0), (0, extra)))
    frac = jnp.pad(shell_frac[0, :, 0].transpose(0, 2, 1), ((0, 0), (0, 0), (0, extra)))
    target = jnp.pad(shell_target[0, 0].T, ((0, 0), (0, extra)), constant_values=64 * 512)
    links = neighbours.transpose(2, 0, 1)
    vmem = pl.BlockSpec(memory_space=pltpu.VMEM)
    result = pl.pallas_call(
        functools.partial(kernel, nb),
        out_shape=jax.ShapeDtypeStruct((8, 64, 512), F32),
        in_specs=[pl.BlockSpec(memory_space=pltpu.HBM)] * 6,
        out_specs=vmem,
        scratch_shapes=[
            pltpu.VMEM((8, 64, 512), F32),
            pltpu.VMEM((1, 64), F32),
            pltpu.VMEM((6, 1, 64), I32),
            pltpu.VMEM((SLOTS, 128), I32),
            pltpu.VMEM((3, SLOTS, 128), F32),
            pltpu.VMEM((SLOTS, 128), I32),
            pltpu.VMEM((8, 128), I32),
            pltpu.SemaphoreType.DMA((6,)),
            pltpu.VMEM((4, 8, 64, 128), F32),
            pltpu.VMEM((512, 1536), BF16),
            pltpu.VMEM((1536, 1024), BF16),
            pltpu.VMEM((512, 1024), F32),
            pltpu.VMEM((256, 128), F32),
            pltpu.VMEM((2, 128, 1, 128), F32),
            pltpu.VMEM((2, 128, 1, 128), F32),
            pltpu.VMEM((4096, 512), BF16),
            pltpu.VMEM((1088, 1024), BF16),
            pltpu.VMEM((1088, 512), F32),
            pltpu.VMEM((3, 4, 9, 64, 128), F32),
            pltpu.VMEM((4, 8, 8, 128), F32),
            pltpu.VMEM((4, 8, 64, 128), F32),
            pltpu.VMEM((6, 256, 128), F32),
            pltpu.VMEM((2, 256, 128), F32),
            pltpu.VMEM((3, 8, 24, 128), F32),
            pltpu.VMEM((STEPS, 3, 8, 24, 128), F32),
            pltpu.VMEM((2, 128, 128), F32),
            pltpu.VMEM((24, 128), I32),
            pltpu.SemaphoreType.DMA((2,)),
            pltpu.SemaphoreType.DMA((2,)),
            pltpu.SemaphoreType.DMA((STEPS, 3, 8)),
            pltpu.SemaphoreType.DMA((STEPS, 3, 8)),
        ],
        compiler_params=pltpu.CompilerParams(
            collective_id=0, has_side_effects=True, vmem_limit_bytes=48 << 20
        ),
    )(*(pltpu.with_memory_space_constraint(x, pltpu.HBM) for x in (conserved[0], block_rate, links, cell, frac, target)))
    return result[None]


def solution(mesh):
    return jax.shard_map(
        functools.partial(on_device, mesh.shape["blk"]),
        mesh=mesh,
        in_specs=(
            P("comp", None, "blk", None),
            P("comp", "blk"),
            P("comp", "blk", None),
            P("comp", "blk", None, None),
            P("comp", None, "blk", None, None),
            P("comp", "blk", None, None),
        ),
        out_specs=P("comp", None, "blk", None),
        check_vma=False,
    )
```

```python
import functools

import jax
import jax.numpy as jnp
from jax import lax
from jax.experimental import pallas as pl
from jax.experimental.pallas import tpu as pltpu
from jax.sharding import PartitionSpec as P

MESH = pl.DeviceIdType.MESH
STEPS = 3
REACH = 4
SLOTS = 32
GAMMA = 5.0 / 3.0
OFFSETS = list(range(-REACH, 0)) + list(range(1, REACH + 1))
SEND_ORDER = sorted(range(2 * REACH), key=lambda o: -abs(OFFSETS[o]))
F32, BF16, I32 = jnp.float32, jnp.bfloat16, jnp.int32


def primitives(u):
    inverse = 1.0 / u[0]
    v = [u[1] * inverse, u[2] * inverse, u[3] * inverse]
    kinetic = 0.5 * (u[1] * v[0] + u[2] * v[1] + u[3] * v[2])
    magnetic = 0.5 * (u[4] * u[4] + u[5] * u[5] + u[6] * u[6])
    pressure = (GAMMA - 1.0) * (u[7] - kinetic - magnetic)
    summed = pressure + magnetic
    align = v[0] * u[4] + v[1] * u[5] + v[2] * u[6]
    sound = GAMMA * pressure * inverse
    combined = sound + 2.0 * magnetic * inverse
    four = 4.0 * sound * inverse
    return v, summed, align, combined, four


def half_flux(u, prim, d):
    v, summed, align, combined, four = prim
    b = u[4:7]
    hn, hb = 0.5 * v[d], 0.5 * b[d]
    flux = [0.5 * u[1 + d]]
    for j in range(3):
        part = u[1 + j] * hn - b[j] * hb
        flux.append(part + 0.5 * summed if j == d else part)
    for j in range(3):
        flux.append(jnp.zeros_like(hn) if j == d else hn * b[j] - hb * v[j])
    flux.append((u[7] + summed) * hn - hb * align)
    inner = jnp.maximum(combined * combined - four * b[d] * b[d], 0.0)
    fast = jnp.sqrt(0.5 * (combined + jnp.sqrt(inner)))
    return flux, jnp.abs(hn) + 0.5 * fast


def take_lanes(table, index):
    rows = table.shape[0]
    return jnp.take_along_axis(
        table, jnp.broadcast_to(index, (rows, 128)), axis=1, mode="promise_in_bounds"
    )


def lane_iota(rows=1):
    return lax.broadcasted_iota(I32, (rows, 128), 1)


def kernel(
    nb, cons_hbm, rate_hbm, nbr_hbm, cell_hbm, frac_hbm, tgt_hbm, out,
    cons, rate, nbr, cell, frac, tgt, links, in_sem,
    cur, ub, wb, tbuf, vbuf, msg_a, msg_b, msg_c, recv_a, recv_b, recv_c, oa, pbuf, acc,
    fs, hy, old, ft, gb, sb, hrecv, rt, idx,
    a_send, a_recv, h_send, h_recv,
):
    comp = lax.axis_index("comp")
    me = lax.axis_index("blk")
    lane = lane_iota()

    def exists(offset):
        return jnp.logical_and(me + offset >= 0, me + offset < nb)

    loads = [
        pltpu.make_async_copy(source, held, in_sem.at[k])
        for k, (source, held) in enumerate(
            ((cell_hbm, cell), (frac_hbm, frac), (cons_hbm, cons), (tgt_hbm, tgt), (nbr_hbm, nbr), (rate_hbm, rate))
        )
    ]
    for load in loads:
        load.start()

    if nb < 128:
        for received in (recv_a, recv_b, recv_c):
            received[...] = jnp.zeros_like(received)
    rt[...] = jnp.zeros_like(rt)

    @pl.loop(0, STEPS)
    def _(s):
        hrecv[s] = jnp.zeros(hrecv.shape[1:], F32)

    barrier = pltpu.get_barrier_semaphore()

    @pl.loop(0, nb)
    def _(q):
        pl.semaphore_signal(barrier, inc=1, device_id=(1 - comp, q), device_id_type=MESH)

    for offset in OFFSETS:
        @pl.when(exists(offset))
        def _():
            pl.semaphore_signal(barrier, inc=1, device_id=(comp, me + offset), device_id_type=MESH)

    for load in loads:
        load.wait()
    for var in range(8):
        for j in range(2):
            low = cons[var, :, 128 * j : 128 * j + 128]
            high = cons[var, :, 128 * j + 256 : 128 * j + 384]
            turned = jnp.concatenate([low, high], axis=0).T
            for k in range(2):
                part = turned[64 * k : 64 * k + 64]
                cur[2 * j + k, var] = part
                upper = part.astype(BF16)
                at = (2 * j + k) * 128
                rows = slice(64 * var, 64 * var + 64)
                ub[rows, at : at + 128] = upper
                ub[rows, at + 512 : at + 640] = (part - upper.astype(F32)).astype(BF16)
                ub[rows, at + 1024 : at + 1152] = upper

    pieces = (((0, 2), msg_a, recv_a), ((2, 3), msg_b, recv_b), ((3, 4), msg_c, recv_c))

    def send_values(piece):
        def send(q):
            pltpu.make_async_remote_copy(
                src_ref=pieces[piece][1].at[q],
                dst_ref=pieces[piece][2].at[me],
                send_sem=a_send.at[piece],
                recv_sem=a_recv.at[piece],
                device_id=(1 - comp, q),
                device_id_type=MESH,
            ).start()

        if nb == 128:
            planes = [
                lax.rem(me // 32 + dx, 4) * 32 + lax.rem(me // 8 + dy, 4) * 8
                for dx, dy in ((2, 2), (2, 1), (2, 3), (1, 2), (3, 2), (1, 1), (1, 3), (3, 1), (3, 3),
                               (2, 0), (0, 2), (1, 0), (3, 0), (0, 1), (0, 3), (0, 0))
            ]
            height = lax.rem(me, 8)

            @pl.loop(0, 8)
            def _(j):
                step = (j + 1) // 2
                z = lax.rem(height + 4 + step * (1 - 2 * lax.rem(j, 2)), 8)
                for plane in planes:
                    send(plane + z)
        else:
            @pl.loop(1, nb + 1)
            def _(i):
                send(lax.rem(me + i, nb))

    rows64 = lax.broadcasted_iota(I32, (64, 128), 0)
    sub8 = lax.broadcasted_iota(I32, (8, 128), 0)

    def interpolate(g):
        at = pl.multiple_of(g * 8, 8)
        cells = cell[pl.ds(at, 8), :]
        fxs, fys, fzs = (frac[k, pl.ds(at, 8), :] for k in range(3))
        xs = (cells >> 6) & 7
        blocks = cells >> 9
        ys, zs = (cells >> 3) & 7, cells & 7

        def along(corners, fractions, row):
            first, part = corners[row], fractions[row]
            return jnp.where(sub8 == first, 1.0 - part, jnp.where(sub8 == first + 1, part, 0.0))

        for t in range(8):
            row = slice(t, t + 1)
            cols = slice(128 * t, 128 * t + 128)
            wx = along(xs, fxs, row)
            upper = wx.astype(BF16).astype(F32)
            lower = wx - upper
            inside = rows64 == blocks[row]
            for x in range(8):
                at = (x & 3) * 128 + (x >> 2) * 64
                part = jnp.where(inside, upper[x : x + 1], 0.0).astype(BF16)
                wb[at : at + 64, cols] = part
                wb[at + 512 : at + 576, cols] = part
                wb[at + 1024 : at + 1088, cols] = jnp.where(inside, lower[x : x + 1], 0.0).astype(BF16)
        tbuf[...] = jnp.dot(ub[...], wb[...], preferred_element_type=F32)
        for t in range(8):
            row = slice(t, t + 1)
            wz = along(zs, fzs, row)
            wy = along(ys, fys, row)
            wys = [wy[y : y + 1] * wz for y in range(8)]
            values = []
            for var in range(8):
                total = None
                for y in range(8):
                    term = wys[y] * tbuf[64 * var + 8 * y : 64 * var + 8 * y + 8, 128 * t : 128 * t + 128]
                    total = term if total is None else total + term
                values.append(jnp.sum(total, axis=0, keepdims=True))
            vbuf[pl.ds(pl.multiple_of(g * 64 + t * 8, 8), 8), :] = jnp.concatenate(values, axis=0)

    for piece, ((first, last), message, _) in enumerate(pieces):
        @pl.loop(first, last)
        def _(g):
            interpolate(g)

        message[...] = vbuf[64 * first : 64 * last, :].T.reshape(message.shape)
        if piece == 0:
            near_by = jnp.minimum(me, REACH) + jnp.minimum(nb - 1 - me, REACH)
            pl.semaphore_wait(barrier, nb + near_by)

        send_values(piece)

    targets = tgt[...]
    tx = (targets >> 6) & 7
    ta = jnp.where(
        targets < 64 * 512, (tx & 3) * 128 + (tx >> 2) * 64 + (targets >> 9), -1
    ).astype(F32)
    columns = jnp.concatenate([ta, jnp.zeros((96, 128), F32)], axis=0).T
    lanes512 = lax.broadcasted_iota(I32, (128, 512), 1).astype(F32)
    for s in range(SLOTS):
        oa[128 * s : 128 * s + 128, :] = jnp.where(
            lanes512 == columns[:, s : s + 1], 1.0, 0.0
        ).astype(BF16)

    links[...] = jnp.full_like(links, -1)
    for f in range(6):
        links[f : f + 1, 0:64] = nbr[f]
        links[f : f + 1, 64:128] = nbr[f]
    links_c = jnp.concatenate([links[...].astype(F32), jnp.zeros((120, 128), F32)], axis=0).T.astype(I32)
    upper_lanes = lane >> 6
    half_lane = lane & 63
    group = (half_lane * 43) >> 8
    place = half_lane - 6 * group
    block_c = lax.broadcasted_iota(I32, (64, 1), 0)
    origin = {}
    for f in range(6):
        near = links[f : f + 1, :]
        far = links_c[0:64, f : f + 1]
        off_r = jnp.where(near >= 0, (near >> 6) - me, 0)
        off_c = jnp.where(far >= 0, (far >> 6) - me, 0)
        before = jnp.where((off_c == off_r) & ((far & 63) < (near & 63)), 1.0, 0.0)
        rank_r = jnp.sum(before, axis=0, keepdims=True).astype(I32)
        earlier = jnp.where((off_c == off_r) & (lane < block_c), 1.0, 0.0)
        rank_c = jnp.sum(earlier, axis=1, keepdims=True).astype(I32)
        slot_c = jnp.where(off_c < 0, off_c + REACH, off_c + REACH - 1)
        slot_c = jnp.where(off_c == 0, -1, slot_c)
        slot_r = jnp.where(off_r < 0, off_r + REACH, off_r + REACH - 1)
        if f < 2:
            wanted = jnp.where(place >= 3, place - 3, place)
            mine = (place >= 3) if f == 1 else (place < 3)
        else:
            wanted = place >> 1
            mine = place >= 0
        hit = (slot_c == group) & (rank_c == wanted) & mine
        which = jnp.sum(jnp.where(hit, block_c.astype(F32), 0.0), axis=0, keepdims=True).astype(I32)
        origin[f] = (off_r, near, rank_r, slot_r, which)
    side = upper_lanes

    def pick(a, b):
        return jnp.where(side == 0, a, b)

    idx[0:1, :] = jnp.where(place >= 3, 64 + origin[1][4], origin[0][4])
    off_x = pick(origin[0][0], origin[1][0])
    near_x = pick(origin[0][1], origin[1][1])
    rank_x = pick(origin[0][2], origin[1][2])
    slot_x = pick(origin[0][3], origin[1][3])
    idx[3:4, :] = jnp.where(near_x >= 0, (1 - side) * 64 + (near_x & 63), lane)
    idx[4:5, :] = jnp.where(off_x != 0, slot_x * 6 + (1 - side) * 3 + rank_x, -1)
    for d in (1, 2):
        idx[d : d + 1, :] = 64 * (place & 1) + pick(origin[2 * d][4], origin[2 * d + 1][4])
        for high in range(2):
            off, near, rank, slot, _ = origin[2 * d + high]
            at = 5 + 6 * (d - 1) + 3 * high
            idx[at : at + 1, :] = jnp.where(near >= 0, 64 * side + (near & 63), -1)
            idx[at + 1 : at + 2, :] = jnp.where(
                off != 0, slot * 6 + rank * 2 + side + (0 if high else 64), -1
            )

    acc[...] = jnp.zeros_like(acc)
    for piece, ((first, last), _, received) in enumerate(pieces):
        whole = received.at[pl.ds(0, nb)]
        pltpu.make_async_copy(whole, whole, a_recv.at[piece]).wait()
        vbuf[64 * first : 64 * last, :] = received[...].reshape(128, 64 * (last - first)).T

        @pl.loop(first, last)
        def _(g):
            places = tgt[pl.ds(pl.multiple_of(g * 8, 8), 8), :] & 63
            for t in range(8):
                value = vbuf[pl.ds(pl.multiple_of(g * 64 + t * 8, 8), 8), :]
                upper = value.astype(BF16).astype(F32)
                lower = value - upper
                here = rows64 == places[t : t + 1]
                cols = slice(128 * t, 128 * t + 128)
                for var in range(8):
                    pbuf[64 * var : 64 * var + 64, cols] = jnp.where(here, upper[var : var + 1], 0.0).astype(BF16)
                    pbuf[512 + 64 * var : 576 + 64 * var, cols] = jnp.where(here, lower[var : var + 1], 0.0).astype(BF16)
            acc[...] += jnp.dot(
                pbuf[...], oa[pl.ds(pl.multiple_of(g * 1024, 1024), 1024), :], preferred_element_type=F32
            )

    for xl in range(4):
        cols = slice(128 * xl, 128 * xl + 128)
        changed = acc[0:64, cols] + acc[512:576, cols] > 0.25
        for var in range(8):
            rows = slice(64 * var, 64 * var + 64)
            lower = slice(512 + 64 * var, 576 + 64 * var)
            cur[xl, var] = jnp.where(changed, acc[rows, cols] + acc[lower, cols], cur[xl, var])
    for piece, (_, message, _) in enumerate(pieces):
        whole = message.at[pl.ds(0, nb)]
        pltpu.make_async_copy(whole, whole, a_send.at[piece]).wait()

    rates = jnp.concatenate([rate[...], rate[...]], axis=1)
    low_lanes = lane_iota(8) < 64
    swap = functools.partial(pltpu.roll, shift=64, axis=1)

    def copy_of(step, pair, o):
        offset = OFFSETS[o]
        return pltpu.make_async_remote_copy(
            src_ref=sb.at[pair, o],
            dst_ref=hrecv.at[step, pair, OFFSETS.index(-offset)],
            send_sem=h_send.at[step, pair, o],
            recv_sem=h_recv.at[step, pair, OFFSETS.index(-offset)],
            device_id=(comp, me + offset),
            device_id_type=MESH,
        )

    def tile(y):
        return pl.ds(pl.multiple_of(y * 8, 8), 8)

    @pl.loop(0, STEPS)
    def _(step):
        for pair in range(3):
            for xl in range(4):
                for var in range(8):
                    at = slice(64 * xl + 8 * var, 64 * xl + 8 * var + 8)
                    if pair == 1:
                        ft[2, at, :] = cur[xl, var, 0:8, :]
                        ft[3, at, :] = cur[xl, var, 56:64, :]
                    elif pair == 2:
                        ft[4, at, :] = cur[xl, var, pl.ds(0, 8, stride=8), :]
                        ft[5, at, :] = cur[xl, var, pl.ds(7, 8, stride=8), :]
            if pair == 0:
                for var in range(8):
                    ft[var // 4, 64 * (var % 4) : 64 * (var % 4) + 64, :] = jnp.where(
                        lane < 64, cur[0, var], cur[3, var]
                    )
            take = idx[pair : pair + 1, :]
            packed = jnp.where(lane < 64, take_lanes(ft[2 * pair], take), take_lanes(ft[2 * pair + 1], take))
            for r in range(2):
                turned = packed[128 * r : 128 * r + 128].T
                for o in range(8):
                    for s in range(2):
                        sb[pair, o, 12 * s + 6 * r : 12 * s + 6 * r + 6, :] = turned[
                            64 * s + 6 * o : 64 * s + 6 * o + 6
                        ]
            for o in SEND_ORDER:
                @pl.when(exists(OFFSETS[o]))
                def _():
                    copy_of(step, pair, o).start()

        @pl.loop(0, 8)
        def _(y):
            for xl in range(4):
                cells = [cur[xl, var, tile(y), :] for var in range(8)]
                for var in range(8):
                    old[xl, var, tile(y), :] = cells[var]
                prim = primitives(cells)
                for d in range(3):
                    flux, speed = half_flux(cells, prim, d)
                    for c in range(8):
                        fs[d, xl, c, tile(y), :] = flux[c]
                    fs[d, xl, 8, tile(y), :] = speed

        hy[...] = jnp.zeros_like(hy)

        @pl.loop(0, 8)
        def _(y):
            here, above = tile(y), tile(jnp.minimum(y + 1, 7))
            keep_y = jnp.where(y < 7, 1.0, 0.0)
            keep_z = sub8 < 7
            sx = [fs[0, xl, 8, here, :] for xl in range(4)]
            mx = [jnp.maximum(sx[xl], sx[xl + 1]) for xl in range(3)]
            mx.append(jnp.maximum(sx[3], swap(sx[0])))
            my, mz = [], []
            for xl in range(4):
                my.append(jnp.maximum(fs[1, xl, 8, here, :], fs[1, xl, 8, above, :]))
                sz = fs[2, xl, 8, here, :]
                mz.append(jnp.maximum(sz, pltpu.roll(sz, 7, 0)))
            for c in range(8):
                state = [old[xl, c, here, :] for xl in range(4)]
                fx = [fs[0, xl, c, here, :] for xl in range(4)]
                hx = []
                for xl in range(3):
                    hx.append(fx[xl] + fx[xl + 1] - mx[xl] * (state[xl + 1] - state[xl]))
                last = fx[3] + swap(fx[0]) - mx[3] * (swap(state[0]) - state[3])
                hx.append(jnp.where(low_lanes, last, 0.0))
                for xl in range(4):
                    change = hx[xl] - (hx[xl - 1] if xl else swap(hx[3]))
                    up = (
                        fs[1, xl, c, here, :] + fs[1, xl, c, above, :]
                        - my[xl] * (old[xl, c, above, :] - state[xl])
                    ) * keep_y
                    change = change + (up - hy[xl, c])
                    hy[xl, c] = up
                    fz = fs[2, xl, c, here, :]
                    right = fz + pltpu.roll(fz, 7, 0) - mz[xl] * (pltpu.roll(state[xl], 7, 0) - state[xl])
                    right = jnp.where(keep_z, right, 0.0)
                    change = change + (right - pltpu.roll(right, 1, 0))
                    cur[xl, c, here, :] = state[xl] - rates * change

        def edge(own, own_flux, own_speed, ghost, d, sign):
            far_flux, far_speed = half_flux(ghost, primitives(ghost), d)
            most = jnp.maximum(own_speed, far_speed)
            return [
                rates * (sign * (own_flux[c] + far_flux[c]) - most * (own[c] - ghost[c]))
                for c in range(8)
            ]

        for s in range(2):
            gb[s] = take_lanes(ft[s], idx[3:4, :])
        for pair in (1, 2):
            for high in range(2):
                at = 5 + 6 * (pair - 1) + 3 * high
                near = idx[at : at + 1, :]
                gb[2 * pair + high] = jnp.where(
                    near >= 0,
                    take_lanes(ft[2 * pair + 1 - high], jnp.maximum(near, 0)),
                    ft[2 * pair + high],
                )

        for pair in range(3):
            for o in range(8):
                @pl.when(exists(-OFFSETS[o]))
                def _():
                    copy_of(step, pair, o).wait_recv()
            for o in range(8):
                for r in range(2):
                    for s in range(2):
                        rt[r, 64 * s + 6 * o : 64 * s + 6 * o + 6, :] = hrecv[
                            step, pair, o, 12 * s + 6 * r : 12 * s + 6 * r + 6, :
                        ]
            arrived = jnp.concatenate([rt[0].T, rt[1].T], axis=0)
            if pair == 0:
                far = idx[4:5, :]
                for s in range(2):
                    gb[s] = jnp.where(
                        far >= 0,
                        take_lanes(arrived, jnp.maximum(far, 0) + 64 * s),
                        gb[s],
                    )

                @pl.loop(0, 8)
                def _(y):
                    own = [ft[c // 4, pl.ds(pl.multiple_of(64 * (c % 4) + y * 8, 8), 8), :] for c in range(8)]
                    ghost = [gb[c // 4, pl.ds(pl.multiple_of(64 * (c % 4) + y * 8, 8), 8), :] for c in range(8)]
                    flux = [jnp.where(low_lanes, fs[0, 0, c, tile(y), :], fs[0, 3, c, tile(y), :]) for c in range(9)]
                    delta = edge(own, flux[:8], flux[8], ghost, 0, jnp.where(low_lanes, 1.0, -1.0))
                    for c in range(8):
                        cur[0, c, tile(y), :] = cur[0, c, tile(y), :] + jnp.where(low_lanes, delta[c], 0.0)
                        cur[3, c, tile(y), :] = cur[3, c, tile(y), :] + jnp.where(low_lanes, 0.0, delta[c])
            else:
                for high in range(2):
                    at = 5 + 6 * (pair - 1) + 3 * high
                    far = idx[at + 1 : at + 2, :]
                    mine = 2 * pair + high
                    gb[mine] = jnp.where(far >= 0, take_lanes(arrived, jnp.maximum(far, 0)), gb[mine])
                    if pair == 1:
                        part = slice(56, 64) if high else slice(0, 8)
                    else:
                        part = pl.ds(7 if high else 0, 8, stride=8)
                    for xl in range(4):
                        rows = [slice(64 * xl + 8 * c, 64 * xl + 8 * c + 8) for c in range(8)]
                        own = [ft[mine, rows[c], :] for c in range(8)]
                        ghost = [gb[mine, rows[c], :] for c in range(8)]
                        flux = [fs[pair, xl, c, part, :] for c in range(9)]
                        delta = edge(own, flux[:8], flux[8], ghost, pair, -1.0 if high else 1.0)
                        for c in range(8):
                            cur[xl, c, part, :] = cur[xl, c, part, :] + delta[c]

        for pair in range(3):
            for o in range(8):
                @pl.when(exists(OFFSETS[o]))
                def _():
                    copy_of(step, pair, o).wait_send()

    for var in range(8):
        for j in range(2):
            turned = jnp.concatenate([cur[2 * j, var], cur[2 * j + 1, var]], axis=0).T
            out[var, :, 128 * j : 128 * j + 128] = turned[0:64]
            out[var, :, 128 * j + 256 : 128 * j + 384] = turned[64:128]


def on_device(nb, conserved, block_rate, neighbours, shell_cell, shell_frac, shell_target):
    extra = 128 - nb
    cell = jnp.pad(shell_cell[0, 0].T, ((0, 0), (0, extra)))
    frac = jnp.pad(shell_frac[0, :, 0].transpose(0, 2, 1), ((0, 0), (0, 0), (0, extra)))
    target = jnp.pad(shell_target[0, 0].T, ((0, 0), (0, extra)), constant_values=64 * 512)
    links = neighbours.transpose(2, 0, 1)
    vmem = pl.BlockSpec(memory_space=pltpu.VMEM)
    result = pl.pallas_call(
        functools.partial(kernel, nb),
        out_shape=jax.ShapeDtypeStruct((8, 64, 512), F32),
        in_specs=[pl.BlockSpec(memory_space=pltpu.HBM)] * 6,
        out_specs=vmem,
        scratch_shapes=[
            pltpu.VMEM((8, 64, 512), F32),
            pltpu.VMEM((1, 64), F32),
            pltpu.VMEM((6, 1, 64), I32),
            pltpu.VMEM((SLOTS, 128), I32),
            pltpu.VMEM((3, SLOTS, 128), F32),
            pltpu.VMEM((SLOTS, 128), I32),
            pltpu.VMEM((8, 128), I32),
            pltpu.SemaphoreType.DMA((6,)),
            pltpu.VMEM((4, 8, 64, 128), F32),
            pltpu.VMEM((512, 1536), BF16),
            pltpu.VMEM((1536, 1024), BF16),
            pltpu.VMEM((512, 1024), F32),
            pltpu.VMEM((256, 128), F32),
            pltpu.VMEM((128, 1, 128), F32),
            pltpu.VMEM((128, 1, 64), F32),
            pltpu.VMEM((128, 1, 64), F32),
            pltpu.VMEM((128, 1, 128), F32),
            pltpu.VMEM((128, 1, 64), F32),
            pltpu.VMEM((128, 1, 64), F32),
            pltpu.VMEM((4096, 512), BF16),
            pltpu.VMEM((1024, 1024), BF16),
            pltpu.VMEM((1024, 512), F32),
            pltpu.VMEM((3, 4, 9, 64, 128), F32),
            pltpu.VMEM((4, 8, 8, 128), F32),
            pltpu.VMEM((4, 8, 64, 128), F32),
            pltpu.VMEM((6, 256, 128), F32),
            pltpu.VMEM((6, 256, 128), F32),
            pltpu.VMEM((3, 8, 24, 128), F32),
            pltpu.VMEM((STEPS, 3, 8, 24, 128), F32),
            pltpu.VMEM((2, 128, 128), F32),
            pltpu.VMEM((24, 128), I32),
            pltpu.SemaphoreType.DMA((3,)),
            pltpu.SemaphoreType.DMA((3,)),
            pltpu.SemaphoreType.DMA((STEPS, 3, 8)),
            pltpu.SemaphoreType.DMA((STEPS, 3, 8)),
        ],
        compiler_params=pltpu.CompilerParams(
            collective_id=0, has_side_effects=True, vmem_limit_bytes=48 << 20
        ),
    )(*(pltpu.with_memory_space_constraint(x, pltpu.HBM) for x in (conserved[0], block_rate, links, cell, frac, target)))
    return result[None]


def solution(mesh):
    return jax.shard_map(
        functools.partial(on_device, mesh.shape["blk"]),
        mesh=mesh,
        in_specs=(
            P("comp", None, "blk", None),
            P("comp", "blk"),
            P("comp", "blk", None),
            P("comp", "blk", None, None),
            P("comp", None, "blk", None, None),
            P("comp", "blk", None, None),
        ),
        out_specs=P("comp", None, "blk", None),
        check_vma=False,
    )
```

```python
import functools

import jax
import jax.numpy as jnp
from jax import lax
from jax.experimental import pallas as pl
from jax.experimental.pallas import tpu as pltpu
from jax.sharding import PartitionSpec as P

MESH = pl.DeviceIdType.MESH
STEPS = 3
REACH = 4
SLOTS = 32
GAMMA = 5.0 / 3.0
OFFSETS = list(range(-REACH, 0)) + list(range(1, REACH + 1))
SEND_ORDER = sorted(range(2 * REACH), key=lambda o: -abs(OFFSETS[o]))
F32, BF16, I32 = jnp.float32, jnp.bfloat16, jnp.int32


def primitives(u):
    inverse = 1.0 / u[0]
    v = [u[1] * inverse, u[2] * inverse, u[3] * inverse]
    kinetic = 0.5 * (u[1] * v[0] + u[2] * v[1] + u[3] * v[2])
    magnetic = 0.5 * (u[4] * u[4] + u[5] * u[5] + u[6] * u[6])
    pressure = (GAMMA - 1.0) * (u[7] - kinetic - magnetic)
    summed = pressure + magnetic
    align = v[0] * u[4] + v[1] * u[5] + v[2] * u[6]
    sound = GAMMA * pressure * inverse
    combined = sound + 2.0 * magnetic * inverse
    four = 4.0 * sound * inverse
    return v, summed, align, combined, four


def half_flux(u, prim, d):
    v, summed, align, combined, four = prim
    b = u[4:7]
    hn, hb = 0.5 * v[d], 0.5 * b[d]
    flux = [0.5 * u[1 + d]]
    for j in range(3):
        part = u[1 + j] * hn - b[j] * hb
        flux.append(part + 0.5 * summed if j == d else part)
    for j in range(3):
        flux.append(jnp.zeros_like(hn) if j == d else hn * b[j] - hb * v[j])
    flux.append((u[7] + summed) * hn - hb * align)
    inner = jnp.maximum(combined * combined - four * b[d] * b[d], 0.0)
    fast = jnp.sqrt(0.5 * (combined + jnp.sqrt(inner)))
    return flux, jnp.abs(hn) + 0.5 * fast


def take_lanes(table, index):
    rows = table.shape[0]
    return jnp.take_along_axis(
        table, jnp.broadcast_to(index, (rows, 128)), axis=1, mode="promise_in_bounds"
    )


def lane_iota(rows=1):
    return lax.broadcasted_iota(I32, (rows, 128), 1)


def kernel(
    nb, cons_hbm, rate_hbm, nbr_hbm, cell_hbm, frac_hbm, tgt_hbm, out,
    cons, rate, nbr, cell, frac, tgt, links, in_sem,
    cur, ub, wb, tbuf, vbuf, msg_a, msg_b, recv_a, recv_b, oa, pbuf, acc,
    fs, hy, old, ft, gb, sb, hrecv, rt, idx,
    a_send, a_recv, h_send, h_recv,
):
    comp = lax.axis_index("comp")
    me = lax.axis_index("blk")
    lane = lane_iota()

    def exists(offset):
        return jnp.logical_and(me + offset >= 0, me + offset < nb)

    loads = [
        pltpu.make_async_copy(source, held, in_sem.at[k])
        for k, (source, held) in enumerate(
            ((cell_hbm, cell), (frac_hbm, frac), (cons_hbm, cons), (tgt_hbm, tgt), (nbr_hbm, nbr), (rate_hbm, rate))
        )
    ]
    for load in loads:
        load.start()

    if nb < 128:
        for received in (recv_a, recv_b):
            received[...] = jnp.zeros_like(received)
    rt[...] = jnp.zeros_like(rt)

    @pl.loop(0, STEPS)
    def _(s):
        hrecv[s] = jnp.zeros(hrecv.shape[1:], F32)

    barrier = pltpu.get_barrier_semaphore()

    @pl.loop(0, nb)
    def _(q):
        pl.semaphore_signal(barrier, inc=1, device_id=(1 - comp, q), device_id_type=MESH)

    for offset in OFFSETS:
        @pl.when(exists(offset))
        def _():
            pl.semaphore_signal(barrier, inc=1, device_id=(comp, me + offset), device_id_type=MESH)

    for load in loads:
        load.wait()
    for var in range(8):
        for j in range(2):
            low = cons[var, :, 128 * j : 128 * j + 128]
            high = cons[var, :, 128 * j + 256 : 128 * j + 384]
            turned = jnp.concatenate([low, high], axis=0).T
            for k in range(2):
                part = turned[64 * k : 64 * k + 64]
                cur[2 * j + k, var] = part
                upper = part.astype(BF16)
                at = (2 * j + k) * 128
                rows = slice(64 * var, 64 * var + 64)
                ub[rows, at : at + 128] = upper
                ub[rows, at + 512 : at + 640] = (part - upper.astype(F32)).astype(BF16)
                ub[rows, at + 1024 : at + 1152] = upper

    pieces = (((0, 2), msg_a, recv_a), ((2, 4), msg_b, recv_b))

    def send_values(piece):
        def send(q):
            pltpu.make_async_remote_copy(
                src_ref=pieces[piece][1].at[q],
                dst_ref=pieces[piece][2].at[me],
                send_sem=a_send.at[piece],
                recv_sem=a_recv.at[piece],
                device_id=(1 - comp, q),
                device_id_type=MESH,
            ).start()

        if nb == 128:
            planes = [
                lax.rem(me // 32 + dx, 4) * 32 + lax.rem(me // 8 + dy, 4) * 8
                for dx, dy in ((2, 2), (2, 1), (2, 3), (1, 2), (3, 2), (1, 1), (1, 3), (3, 1), (3, 3),
                               (2, 0), (0, 2), (1, 0), (3, 0), (0, 1), (0, 3), (0, 0))
            ]
            height = lax.rem(me, 8)

            @pl.loop(0, 8)
            def _(j):
                step = (j + 1) // 2
                z = lax.rem(height + 4 + step * (1 - 2 * lax.rem(j, 2)), 8)
                for plane in planes:
                    send(plane + z)
        else:
            @pl.loop(1, nb + 1)
            def _(i):
                send(lax.rem(me + i, nb))

    rows64 = lax.broadcasted_iota(I32, (64, 128), 0)
    sub8 = lax.broadcasted_iota(I32, (8, 128), 0)

    def interpolate(g):
        at = pl.multiple_of(g * 8, 8)
        cells = cell[pl.ds(at, 8), :]
        fxs, fys, fzs = (frac[k, pl.ds(at, 8), :] for k in range(3))
        xs = (cells >> 6) & 7
        blocks = cells >> 9
        ys, zs = (cells >> 3) & 7, cells & 7

        def along(corners, fractions, row):
            first, part = corners[row], fractions[row]
            return jnp.where(sub8 == first, 1.0 - part, jnp.where(sub8 == first + 1, part, 0.0))

        for t in range(8):
            row = slice(t, t + 1)
            cols = slice(128 * t, 128 * t + 128)
            wx = along(xs, fxs, row)
            upper = wx.astype(BF16).astype(F32)
            lower = wx - upper
            inside = rows64 == blocks[row]
            for x in range(8):
                at = (x & 3) * 128 + (x >> 2) * 64
                part = jnp.where(inside, upper[x : x + 1], 0.0).astype(BF16)
                wb[at : at + 64, cols] = part
                wb[at + 512 : at + 576, cols] = part
                wb[at + 1024 : at + 1088, cols] = jnp.where(inside, lower[x : x + 1], 0.0).astype(BF16)
        tbuf[...] = jnp.dot(ub[...], wb[...], preferred_element_type=F32)
        for t in range(8):
            row = slice(t, t + 1)
            wz = along(zs, fzs, row)
            wy = along(ys, fys, row)
            wys = [wy[y : y + 1] * wz for y in range(8)]
            values = []
            for var in range(8):
                total = None
                for y in range(8):
                    term = wys[y] * tbuf[64 * var + 8 * y : 64 * var + 8 * y + 8, 128 * t : 128 * t + 128]
                    total = term if total is None else total + term
                values.append(jnp.sum(total, axis=0, keepdims=True))
            vbuf[pl.ds(pl.multiple_of(g * 64 + t * 8, 8), 8), :] = jnp.concatenate(values, axis=0)

    @pl.loop(0, 4)
    def _(g):
        interpolate(g)
        for piece, ((first, last), message, _) in enumerate(pieces):
            @pl.when(g == last - 1)
            def _():
                message[...] = vbuf[64 * first : 64 * last, :].T.reshape(message.shape)
                if piece == 0:
                    near_by = jnp.minimum(me, REACH) + jnp.minimum(nb - 1 - me, REACH)
                    pl.semaphore_wait(barrier, nb + near_by)
                send_values(piece)

    targets = tgt[...]
    tx = (targets >> 6) & 7
    ta = jnp.where(
        targets < 64 * 512, (tx & 3) * 128 + (tx >> 2) * 64 + (targets >> 9), -1
    ).astype(F32)
    columns = jnp.concatenate([ta, jnp.zeros((96, 128), F32)], axis=0).T
    lanes512 = lax.broadcasted_iota(I32, (128, 512), 1).astype(F32)
    for s in range(SLOTS):
        oa[128 * s : 128 * s + 128, :] = jnp.where(
            lanes512 == columns[:, s : s + 1], 1.0, 0.0
        ).astype(BF16)

    links[...] = jnp.full_like(links, -1)
    for f in range(6):
        links[f : f + 1, 0:64] = nbr[f]
        links[f : f + 1, 64:128] = nbr[f]
    links_c = jnp.concatenate([links[...].astype(F32), jnp.zeros((120, 128), F32)], axis=0).T.astype(I32)
    upper_lanes = lane >> 6
    half_lane = lane & 63
    group = (half_lane * 43) >> 8
    place = half_lane - 6 * group
    block_c = lax.broadcasted_iota(I32, (64, 1), 0)
    origin = {}
    for f in range(6):
        near = links[f : f + 1, :]
        far = links_c[0:64, f : f + 1]
        off_r = jnp.where(near >= 0, (near >> 6) - me, 0)
        off_c = jnp.where(far >= 0, (far >> 6) - me, 0)
        before = jnp.where((off_c == off_r) & ((far & 63) < (near & 63)), 1.0, 0.0)
        rank_r = jnp.sum(before, axis=0, keepdims=True).astype(I32)
        earlier = jnp.where((off_c == off_r) & (lane < block_c), 1.0, 0.0)
        rank_c = jnp.sum(earlier, axis=1, keepdims=True).astype(I32)
        slot_c = jnp.where(off_c < 0, off_c + REACH, off_c + REACH - 1)
        slot_c = jnp.where(off_c == 0, -1, slot_c)
        slot_r = jnp.where(off_r < 0, off_r + REACH, off_r + REACH - 1)
        if f < 2:
            wanted = jnp.where(place >= 3, place - 3, place)
            mine = (place >= 3) if f == 1 else (place < 3)
        else:
            wanted = place >> 1
            mine = place >= 0
        hit = (slot_c == group) & (rank_c == wanted) & mine
        which = jnp.sum(jnp.where(hit, block_c.astype(F32), 0.0), axis=0, keepdims=True).astype(I32)
        origin[f] = (off_r, near, rank_r, slot_r, which)
    side = upper_lanes

    def pick(a, b):
        return jnp.where(side == 0, a, b)

    idx[0:1, :] = jnp.where(place >= 3, 64 + origin[1][4], origin[0][4])
    off_x = pick(origin[0][0], origin[1][0])
    near_x = pick(origin[0][1], origin[1][1])
    rank_x = pick(origin[0][2], origin[1][2])
    slot_x = pick(origin[0][3], origin[1][3])
    idx[3:4, :] = jnp.where(near_x >= 0, (1 - side) * 64 + (near_x & 63), lane)
    idx[4:5, :] = jnp.where(off_x != 0, slot_x * 6 + (1 - side) * 3 + rank_x, -1)
    for d in (1, 2):
        idx[d : d + 1, :] = 64 * (place & 1) + pick(origin[2 * d][4], origin[2 * d + 1][4])
        for high in range(2):
            off, near, rank, slot, _ = origin[2 * d + high]
            at = 5 + 6 * (d - 1) + 3 * high
            idx[at : at + 1, :] = jnp.where(near >= 0, 64 * side + (near & 63), -1)
            idx[at + 1 : at + 2, :] = jnp.where(
                off != 0, slot * 6 + rank * 2 + side + (0 if high else 64), -1
            )

    acc[...] = jnp.zeros_like(acc)
    @pl.loop(0, 4)
    def _(g):
        for piece, ((first, last), _, received) in enumerate(pieces):
            @pl.when(g == first)
            def _():
                whole = received.at[pl.ds(0, nb)]
                pltpu.make_async_copy(whole, whole, a_recv.at[piece]).wait()
                vbuf[64 * first : 64 * last, :] = received[...].reshape(128, 64 * (last - first)).T

        places = tgt[pl.ds(pl.multiple_of(g * 8, 8), 8), :] & 63
        for t in range(8):
            value = vbuf[pl.ds(pl.multiple_of(g * 64 + t * 8, 8), 8), :]
            upper = value.astype(BF16).astype(F32)
            lower = value - upper
            here = rows64 == places[t : t + 1]
            cols = slice(128 * t, 128 * t + 128)
            for var in range(8):
                pbuf[64 * var : 64 * var + 64, cols] = jnp.where(here, upper[var : var + 1], 0.0).astype(BF16)
                pbuf[512 + 64 * var : 576 + 64 * var, cols] = jnp.where(here, lower[var : var + 1], 0.0).astype(BF16)
        acc[...] += jnp.dot(
            pbuf[...], oa[pl.ds(pl.multiple_of(g * 1024, 1024), 1024), :], preferred_element_type=F32
        )

    for xl in range(4):
        cols = slice(128 * xl, 128 * xl + 128)
        changed = acc[0:64, cols] + acc[512:576, cols] > 0.25
        for var in range(8):
            rows = slice(64 * var, 64 * var + 64)
            lower = slice(512 + 64 * var, 576 + 64 * var)
            cur[xl, var] = jnp.where(changed, acc[rows, cols] + acc[lower, cols], cur[xl, var])
    for piece, (_, message, _) in enumerate(pieces):
        whole = message.at[pl.ds(0, nb)]
        pltpu.make_async_copy(whole, whole, a_send.at[piece]).wait()

    rates = jnp.concatenate([rate[...], rate[...]], axis=1)
    low_lanes = lane_iota(8) < 64
    swap = functools.partial(pltpu.roll, shift=64, axis=1)

    def copy_of(step, pair, o):
        offset = OFFSETS[o]
        return pltpu.make_async_remote_copy(
            src_ref=sb.at[step, pair, o],
            dst_ref=hrecv.at[step, pair, OFFSETS.index(-offset)],
            send_sem=h_send.at[step, pair, o],
            recv_sem=h_recv.at[step, pair, OFFSETS.index(-offset)],
            device_id=(comp, me + offset),
            device_id_type=MESH,
        )

    def sent(step):
        for pair in range(3):
            for o in range(8):
                @pl.when(exists(OFFSETS[o]))
                def _():
                    copy_of(step, pair, o).wait_send()

    def tile(y):
        return pl.ds(pl.multiple_of(y * 8, 8), 8)

    @pl.loop(0, STEPS)
    def _(step):
        for pair in range(3):
            for xl in range(4):
                for var in range(8):
                    at = slice(64 * xl + 8 * var, 64 * xl + 8 * var + 8)
                    if pair == 1:
                        ft[2, at, :] = cur[xl, var, 0:8, :]
                        ft[3, at, :] = cur[xl, var, 56:64, :]
                    elif pair == 2:
                        ft[4, at, :] = cur[xl, var, pl.ds(0, 8, stride=8), :]
                        ft[5, at, :] = cur[xl, var, pl.ds(7, 8, stride=8), :]
            if pair == 0:
                for var in range(8):
                    ft[var // 4, 64 * (var % 4) : 64 * (var % 4) + 64, :] = jnp.where(
                        lane < 64, cur[0, var], cur[3, var]
                    )
            take = idx[pair : pair + 1, :]
            packed = jnp.where(lane < 64, take_lanes(ft[2 * pair], take), take_lanes(ft[2 * pair + 1], take))
            for r in range(2):
                turned = packed[128 * r : 128 * r + 128].T
                for o in range(8):
                    for s in range(2):
                        sb[step, pair, o, 12 * s + 6 * r : 12 * s + 6 * r + 6, :] = turned[
                            64 * s + 6 * o : 64 * s + 6 * o + 6
                        ]
            for o in SEND_ORDER:
                @pl.when(exists(OFFSETS[o]))
                def _():
                    copy_of(step, pair, o).start()

        @pl.loop(0, 8)
        def _(y):
            for xl in range(4):
                cells = [cur[xl, var, tile(y), :] for var in range(8)]
                for var in range(8):
                    old[xl, var, tile(y), :] = cells[var]
                prim = primitives(cells)
                for d in range(3):
                    flux, speed = half_flux(cells, prim, d)
                    for c in range(8):
                        fs[d, xl, c, tile(y), :] = flux[c]
                    fs[d, xl, 8, tile(y), :] = speed

        hy[...] = jnp.zeros_like(hy)

        @pl.loop(0, 8)
        def _(y):
            here, above = tile(y), tile(jnp.minimum(y + 1, 7))
            keep_y = jnp.where(y < 7, 1.0, 0.0)
            keep_z = sub8 < 7
            sx = [fs[0, xl, 8, here, :] for xl in range(4)]
            mx = [jnp.maximum(sx[xl], sx[xl + 1]) for xl in range(3)]
            mx.append(jnp.maximum(sx[3], swap(sx[0])))
            my, mz = [], []
            for xl in range(4):
                my.append(jnp.maximum(fs[1, xl, 8, here, :], fs[1, xl, 8, above, :]))
                sz = fs[2, xl, 8, here, :]
                mz.append(jnp.maximum(sz, pltpu.roll(sz, 7, 0)))
            for c in range(8):
                state = [old[xl, c, here, :] for xl in range(4)]
                fx = [fs[0, xl, c, here, :] for xl in range(4)]
                hx = []
                for xl in range(3):
                    hx.append(fx[xl] + fx[xl + 1] - mx[xl] * (state[xl + 1] - state[xl]))
                last = fx[3] + swap(fx[0]) - mx[3] * (swap(state[0]) - state[3])
                hx.append(jnp.where(low_lanes, last, 0.0))
                for xl in range(4):
                    change = hx[xl] - (hx[xl - 1] if xl else swap(hx[3]))
                    up = (
                        fs[1, xl, c, here, :] + fs[1, xl, c, above, :]
                        - my[xl] * (old[xl, c, above, :] - state[xl])
                    ) * keep_y
                    change = change + (up - hy[xl, c])
                    hy[xl, c] = up
                    fz = fs[2, xl, c, here, :]
                    right = fz + pltpu.roll(fz, 7, 0) - mz[xl] * (pltpu.roll(state[xl], 7, 0) - state[xl])
                    right = jnp.where(keep_z, right, 0.0)
                    change = change + (right - pltpu.roll(right, 1, 0))
                    cur[xl, c, here, :] = state[xl] - rates * change

        def edge(own, own_flux, own_speed, ghost, d, sign):
            far_flux, far_speed = half_flux(ghost, primitives(ghost), d)
            most = jnp.maximum(own_speed, far_speed)
            return [
                rates * (sign * (own_flux[c] + far_flux[c]) - most * (own[c] - ghost[c]))
                for c in range(8)
            ]

        @pl.when(step > 0)
        def _():
            sent(step - 1)

        for s in range(2):
            gb[s] = take_lanes(ft[s], idx[3:4, :])
        for pair in (1, 2):
            for high in range(2):
                at = 5 + 6 * (pair - 1) + 3 * high
                near = idx[at : at + 1, :]
                gb[2 * pair + high] = jnp.where(
                    near >= 0,
                    take_lanes(ft[2 * pair + 1 - high], jnp.maximum(near, 0)),
                    ft[2 * pair + high],
                )

        for pair in range(3):
            for o in range(8):
                @pl.when(exists(-OFFSETS[o]))
                def _():
                    copy_of(step, pair, o).wait_recv()
            for o in range(8):
                for r in range(2):
                    for s in range(2):
                        rt[r, 64 * s + 6 * o : 64 * s + 6 * o + 6, :] = hrecv[
                            step, pair, o, 12 * s + 6 * r : 12 * s + 6 * r + 6, :
                        ]
            arrived = jnp.concatenate([rt[0].T, rt[1].T], axis=0)
            if pair == 0:
                far = idx[4:5, :]
                for s in range(2):
                    gb[s] = jnp.where(
                        far >= 0,
                        take_lanes(arrived, jnp.maximum(far, 0) + 64 * s),
                        gb[s],
                    )

                @pl.loop(0, 8)
                def _(y):
                    own = [ft[c // 4, pl.ds(pl.multiple_of(64 * (c % 4) + y * 8, 8), 8), :] for c in range(8)]
                    ghost = [gb[c // 4, pl.ds(pl.multiple_of(64 * (c % 4) + y * 8, 8), 8), :] for c in range(8)]
                    flux = [jnp.where(low_lanes, fs[0, 0, c, tile(y), :], fs[0, 3, c, tile(y), :]) for c in range(9)]
                    delta = edge(own, flux[:8], flux[8], ghost, 0, jnp.where(low_lanes, 1.0, -1.0))
                    for c in range(8):
                        cur[0, c, tile(y), :] = cur[0, c, tile(y), :] + jnp.where(low_lanes, delta[c], 0.0)
                        cur[3, c, tile(y), :] = cur[3, c, tile(y), :] + jnp.where(low_lanes, 0.0, delta[c])
            else:
                for high in range(2):
                    at = 5 + 6 * (pair - 1) + 3 * high
                    far = idx[at + 1 : at + 2, :]
                    mine = 2 * pair + high
                    gb[mine] = jnp.where(far >= 0, take_lanes(arrived, jnp.maximum(far, 0)), gb[mine])
                    if pair == 1:
                        part = slice(56, 64) if high else slice(0, 8)
                    else:
                        part = pl.ds(7 if high else 0, 8, stride=8)
                    for xl in range(4):
                        rows = [slice(64 * xl + 8 * c, 64 * xl + 8 * c + 8) for c in range(8)]
                        own = [ft[mine, rows[c], :] for c in range(8)]
                        ghost = [gb[mine, rows[c], :] for c in range(8)]
                        flux = [fs[pair, xl, c, part, :] for c in range(9)]
                        delta = edge(own, flux[:8], flux[8], ghost, pair, -1.0 if high else 1.0)
                        for c in range(8):
                            cur[xl, c, part, :] = cur[xl, c, part, :] + delta[c]

    sent(STEPS - 1)

    for var in range(8):
        for j in range(2):
            turned = jnp.concatenate([cur[2 * j, var], cur[2 * j + 1, var]], axis=0).T
            out[var, :, 128 * j : 128 * j + 128] = turned[0:64]
            out[var, :, 128 * j + 256 : 128 * j + 384] = turned[64:128]


def on_device(nb, conserved, block_rate, neighbours, shell_cell, shell_frac, shell_target):
    extra = 128 - nb
    cell = jnp.pad(shell_cell[0, 0].T, ((0, 0), (0, extra)))
    frac = jnp.pad(shell_frac[0, :, 0].transpose(0, 2, 1), ((0, 0), (0, 0), (0, extra)))
    target = jnp.pad(shell_target[0, 0].T, ((0, 0), (0, extra)), constant_values=64 * 512)
    links = neighbours.transpose(2, 0, 1)
    vmem = pl.BlockSpec(memory_space=pltpu.VMEM)
    result = pl.pallas_call(
        functools.partial(kernel, nb),
        out_shape=jax.ShapeDtypeStruct((8, 64, 512), F32),
        in_specs=[pl.BlockSpec(memory_space=pltpu.HBM)] * 6,
        out_specs=vmem,
        scratch_shapes=[
            pltpu.VMEM((8, 64, 512), F32),
            pltpu.VMEM((1, 64), F32),
            pltpu.VMEM((6, 1, 64), I32),
            pltpu.VMEM((SLOTS, 128), I32),
            pltpu.VMEM((3, SLOTS, 128), F32),
            pltpu.VMEM((SLOTS, 128), I32),
            pltpu.VMEM((8, 128), I32),
            pltpu.SemaphoreType.DMA((6,)),
            pltpu.VMEM((4, 8, 64, 128), F32),
            pltpu.VMEM((512, 1536), BF16),
            pltpu.VMEM((1536, 1024), BF16),
            pltpu.VMEM((512, 1024), F32),
            pltpu.VMEM((256, 128), F32),
            pltpu.VMEM((128, 1, 128), F32),
            pltpu.VMEM((128, 1, 128), F32),
            pltpu.VMEM((128, 1, 128), F32),
            pltpu.VMEM((128, 1, 128), F32),
            pltpu.VMEM((4096, 512), BF16),
            pltpu.VMEM((1024, 1024), BF16),
            pltpu.VMEM((1024, 512), F32),
            pltpu.VMEM((3, 4, 9, 64, 128), F32),
            pltpu.VMEM((4, 8, 8, 128), F32),
            pltpu.VMEM((4, 8, 64, 128), F32),
            pltpu.VMEM((6, 256, 128), F32),
            pltpu.VMEM((6, 256, 128), F32),
            pltpu.VMEM((STEPS, 3, 8, 24, 128), F32),
            pltpu.VMEM((STEPS, 3, 8, 24, 128), F32),
            pltpu.VMEM((2, 128, 128), F32),
            pltpu.VMEM((24, 128), I32),
            pltpu.SemaphoreType.DMA((2,)),
            pltpu.SemaphoreType.DMA((2,)),
            pltpu.SemaphoreType.DMA((STEPS, 3, 8)),
            pltpu.SemaphoreType.DMA((STEPS, 3, 8)),
        ],
        compiler_params=pltpu.CompilerParams(
            collective_id=0, has_side_effects=True, vmem_limit_bytes=48 << 20
        ),
    )(*(pltpu.with_memory_space_constraint(x, pltpu.HBM) for x in (conserved[0], block_rate, links, cell, frac, target)))
    return result[None]


def solution(mesh):
    return jax.shard_map(
        functools.partial(on_device, mesh.shape["blk"]),
        mesh=mesh,
        in_specs=(
            P("comp", None, "blk", None),
            P("comp", "blk"),
            P("comp", "blk", None),
            P("comp", "blk", None, None),
            P("comp", None, "blk", None, None),
            P("comp", "blk", None, None),
        ),
        out_specs=P("comp", None, "blk", None),
        check_vma=False,
    )
```
